32 devices in a mesh: chain: 16 (over z, y, x), grp: 2 (over core).
Axes of the slice: x: 2, y: 2, z: 4, core: 2. Of those that a mesh axis runs over, the one named last changes fastest.
Arguments:
- right_side: float32 [32, 64, 1024], P(('chain', 'grp')), may hold values from -6 to 6
- start: float32 [32, 64, 1024], P(('chain', 'grp')), may hold values from -3 to 3
- diag_tiles: float32 [32, 1024, 1024], P(('chain', 'grp')), may hold values from -0.12 to 2.92, as said below
- neighbour_tiles: float32 [32, 1024, 1024], P(('chain', 'grp')), may hold values from -0.0234375 to 0.0234375
- factors: float32 [32, 28, 96, 1024], P(('chain', 'grp')), may hold values from -0.078125 to 0.078125
- partner: int32 [32, 28], P(('chain', 'grp')), may hold values from -1 to 31, as said below
- ranks: int32 [32, 28], P(('chain', 'grp')), may hold values from 0 to 96, as said below
Outputs:
- solution: float32 [32, 64, 1024], P(('chain', 'grp'))
- residual: float32 [32, 64, 1024], P(('chain', 'grp'))
The draws below stay inside these ranges and needn't reach their ends.
Inputs may be any that keep to these rules, and one draw needn't show every extreme that they name: If partner[i, s] = j >= 0 then j is not i, i - 1 or i + 1, partner[j, s] = i and ranks[j, s] = ranks[i, s]; no two slots of one cluster name the same partner; cluster 0 and cluster 32 - 1 are a far pair. ranks is 0 exactly at empty slots and from 32 to 96 elsewhere; every pair of cluster 0 has rank 96. `diag_tiles`: every tile is symmetric.
All inputs are finite; a program needn't handle non-finite values.
Results may differ from the reference program's by a relative error of at most 0.00017.
Values sent between devices are 32-bit elements; how exact they have to be, the bound alone decides.
No kernel may reach another device: no remote copies, remote signals or barrier semaphores. Data moves between devices by JAX's collectives and lax.ppermute only.
A program may use at most 128 MiB of HBM per device.

```python
import jax
import jax.numpy as jnp
from jax import lax

CS = 1024
NRHS = 64
RMAX = 96
ITERS = 2
CLUSTERS = 32
SLOTS = 28


def swap_places(values, first, second):
    first_value = values[first]
    second_value = values[second]
    return values.at[first].set(second_value).at[second].set(first_value)


def pair_graph(key):
    base = jax.random.fold_in(key, 7)
    key_label, key_rounds, key_rank = jax.random.split(base, 3)
    chosen = jax.random.permutation(key_rounds, CLUSTERS - 1)[:SLOTS].astype(jnp.int32)
    last_label = CLUSTERS - 1
    labels_of = jax.random.permutation(key_label, CLUSTERS).astype(jnp.int32)
    where_last = jnp.argmax((labels_of == last_label).astype(jnp.int32)).astype(jnp.int32)
    labels_of = swap_places(labels_of, jnp.int32(0), where_last)
    where_round = jnp.argmax((labels_of == chosen[0]).astype(jnp.int32)).astype(jnp.int32)
    labels_of = swap_places(labels_of, jnp.int32(CLUSTERS - 1), where_round)
    own_index = jnp.arange(CLUSTERS, dtype=jnp.int32)
    inverse = jnp.zeros((CLUSTERS,), jnp.int32).at[labels_of].set(own_index)
    rounds = chosen[:, None]
    own_label = labels_of[None, :]
    circle_label = jnp.mod(2 * rounds - own_label, last_label).astype(jnp.int32)
    paired_label = jnp.where(own_label == last_label, rounds, jnp.where(own_label == rounds, last_label, circle_label))
    mate_of = inverse[paired_label.astype(jnp.int32)]
    kept_pair = jnp.abs(mate_of - own_index[None, :]) > 1
    partner = jnp.where(kept_pair, mate_of, -1).T
    rank_table = jax.random.randint(key_rank, (SLOTS, CLUSTERS), RMAX // 3, RMAX + 1)
    rank_table = rank_table.at[:, 0].set(RMAX)
    low_end = jnp.minimum(mate_of, own_index[None, :]).astype(jnp.int32)
    pair_rank = jnp.take_along_axis(rank_table, low_end, axis=1)
    ranks = jnp.where(kept_pair, pair_rank, 0).T
    return (partner.astype(jnp.int32), ranks.astype(jnp.int32))


def draw_partner(key, part):
    return pair_graph(key)[0]


def draw_ranks(key, part):
    return pair_graph(key)[1]


def draw_diag_tiles(key, part):
    key_noise, key_diagonal = jax.random.split(jax.random.fold_in(key, 11))
    noise_draw = jnp.clip(jax.random.normal(key_noise, (CLUSTERS, CS, CS), jnp.float32), -4.0, 4.0)
    diagonal_values = jnp.exp(jax.random.uniform(key_diagonal, (CLUSTERS, CS), jnp.float32, jnp.log(1.5), jnp.log(2.8)))
    symmetric = (noise_draw + jnp.swapaxes(noise_draw, 1, 2)) * (0.15 / jnp.sqrt(2.0 * CS))
    identity = jnp.eye(CS, dtype=jnp.float32)[None, :, :]
    return (symmetric + identity * diagonal_values[:, None, :]).astype(jnp.float32)


def levels(key, dims, cuts, smallest, largest):
    def one(dim, blocks):
        heights = jax.random.uniform(jax.random.fold_in(jax.random.fold_in(key, 6), dim), (blocks,), jnp.float32, smallest / len(cuts), largest / len(cuts))
        return jnp.repeat(jnp.exp(heights), dims[dim] // blocks).reshape((-1,) + (1,) * (len(dims) - dim - 1))

    gain = one(*cuts[0])
    for cut in cuts[1:]:
        gain = gain * one(*cut)
    return gain


def normal_values(rng, shape, width, reach, cuts=(), held_as=jnp.bfloat16):
    gain = levels(rng, shape, cuts, -0.22, 0.18) if cuts else 1.0
    array = jax.random.normal(rng, shape, jnp.float32) * width * gain
    return jnp.minimum(jnp.maximum(array, -reach), reach).astype(held_as)


def setup_inputs(seed: int = 0) -> dict:
    key_of = jax.random.split(jax.random.key(seed), 8)
    return {
        "right_side": normal_values(key_of[0], (CLUSTERS, NRHS, CS), 1.0, 6.0, ((0, 32),), jnp.float32),
        "start": normal_values(key_of[1], (CLUSTERS, NRHS, CS), 0.5, 3.0, ((0, 32),), jnp.float32),
        "diag_tiles": draw_diag_tiles(jax.random.fold_in(key_of[7], 71), 0),
        "neighbour_tiles": normal_values(key_of[3], (CLUSTERS, CS, CS), (64 * CS) ** -0.5, 0.0234375, ((0, 32),), jnp.float32),
        "factors": normal_values(key_of[4], (CLUSTERS, SLOTS, RMAX, CS), (6 * CS) ** -0.5, 0.078125, ((0, 32),), jnp.float32),
        "partner": draw_partner(jax.random.fold_in(key_of[7], 71), 0),
        "ranks": draw_ranks(jax.random.fold_in(key_of[7], 71), 0),
    }


exact_mode = lax.Precision.HIGHEST
spectrum_low = 0.7
spectrum_high = 3.6


def apply_matrix(vectors, diag_tiles, neighbour_tiles, masked_factors, partner):
    local_term = jnp.einsum("inc,idc->ind", vectors, diag_tiles, precision=exact_mode)
    following = jnp.concatenate([vectors[1:], jnp.zeros_like(vectors[:1])], axis=0)
    upper_term = jnp.einsum("inc,idc->ind", following, neighbour_tiles, precision=exact_mode)
    carried = jnp.einsum("inc,icd->ind", vectors, neighbour_tiles, precision=exact_mode)
    lower_term = jnp.concatenate([jnp.zeros_like(carried[:1]), carried[:-1]], axis=0)
    projected = jnp.einsum("inc,isrc->isnr", vectors, masked_factors, precision=exact_mode)
    slot_index = jnp.arange(partner.shape[1], dtype=jnp.int32)[None, :]
    fetched = projected[jnp.maximum(partner, 0).astype(jnp.int32), slot_index]
    fetched = jnp.where((partner >= 0)[:, :, None, None], fetched, jnp.zeros_like(fetched))
    far_term = jnp.einsum("isnr,isrc->inc", fetched, masked_factors, precision=exact_mode)
    return local_term + upper_term + lower_term + far_term


def reference(right_side, start, diag_tiles, neighbour_tiles, factors, partner, ranks):
    rank_mask = (jnp.arange(factors.shape[2], dtype=jnp.int32)[None, None, :] < ranks[:, :, None]).astype(factors.dtype)
    masked_factors = factors * rank_mask[:, :, :, None]
    center = (spectrum_low + spectrum_high) / 2.0
    half_width = (spectrum_high - spectrum_low) / 2.0
    ratio = center / half_width
    rho_now = 1.0 / ratio
    solution = start
    residual = right_side - apply_matrix(start, diag_tiles, neighbour_tiles, masked_factors, partner)
    direction = residual / center
    for iteration in range(ITERS):
        solution = solution + direction
        residual = residual - apply_matrix(direction, diag_tiles, neighbour_tiles, masked_factors, partner)
        if iteration + 1 < ITERS:
            rho_next = 1.0 / (2.0 * ratio - rho_now)
            direction = (rho_next * rho_now) * direction + (2.0 * rho_next / half_width) * residual
            rho_now = rho_next
    return solution, residual
```

```python
import functools

import jax
import jax.numpy as jnp
from jax import lax
from jax.experimental import pallas as pl
from jax.experimental.pallas import tpu as pltpu
from jax.sharding import PartitionSpec as P


ITERS = 2

spectrum_low = 0.7
spectrum_high = 3.6

AXES = ("chain", "grp")
NT = (((1,), (1,)), ((), ()))
NN = (((1,), (0,)), ((), ()))
TN = (((0,), (0,)), ((), ()))
VMEM_LIMIT = 40 * 1024 * 1024
STEPS = 4


def from_behind(block, distance):
    devices = range(lax.axis_size(AXES))
    route = [(i - distance, i) for i in devices if i - distance in devices]
    return lax.ppermute(block, AXES, route)


def halves(value):
    high = value.astype(jnp.bfloat16)
    low = (value - high.astype(jnp.float32)).astype(jnp.bfloat16)
    return high, low


def product(left, right, form):
    return lax.dot_general(left, right, form, preferred_element_type=jnp.float32)


class Loader:
    def __init__(self, factors_ref, buffer, semaphore, high_ref=None, low_ref=None):
        self.factors_ref, self.buffer, self.semaphore = factors_ref, buffer, semaphore
        self.high_ref, self.low_ref = high_ref, low_ref
        self.width = factors_ref.shape[1]
        slots = factors_ref.shape[0]
        size = -(-slots // STEPS)
        self.groups = [(at, min(size, slots - at)) for at in range(0, slots, size)]

    def copy(self, index):
        at, size = self.groups[index]
        return pltpu.make_async_copy(
            self.factors_ref.at[at:at + size], self.buffer.at[at:at + size],
            self.semaphore.at[index],
        )

    def start(self):
        for index in range(len(self.groups)):
            self.copy(index).start()

    def rows(self, at, size):
        return slice(at * self.width, (at + size) * self.width)

    def parts(self):
        for index, (at, size) in enumerate(self.groups):
            self.copy(index).wait()
            rows = self.buffer[at:at + size].reshape(size * self.width, self.buffer.shape[2])
            high, low = halves(rows)
            if self.high_ref is not None:
                self.high_ref[self.rows(at, size), :] = high
                self.low_ref[self.rows(at, size), :] = low
            yield at, size, high, low

    def kept(self):
        for at, size in self.groups:
            rows = self.rows(at, size)
            yield at, size, self.high_ref[rows, :], self.low_ref[rows, :]


def project(parts, width, vectors, partner_ref, ranks_ref, outgoing_ref):
    high, low = halves(vectors)
    operand = jnp.concatenate([high, low], axis=0)
    lanes = operand.shape[0]
    half = width // 2
    left = lax.broadcasted_iota(jnp.int32, (half, lanes), 1) < lanes // 2
    rank_index = lax.broadcasted_iota(jnp.int32, (half, lanes), 0) + jnp.where(left, 0, half)
    for at, size, factor_high, factor_low in parts:
        rows = product(factor_high, operand, NT) + product(factor_low, operand, NT)
        rows = rows + pltpu.roll(rows, lanes // 2, 1)
        for inner in range(size):
            base = inner * width
            chunk = jnp.where(left, rows[base:base + half], rows[base + half:base + width])
            slot = at + inner
            chunk = jnp.where(rank_index < ranks_ref[slot], chunk, 0.0)
            place = partner_ref[slot]

            @pl.when(place >= 0)
            def _():
                outgoing_ref[place] = chunk


def unpack(width, slots, partner_ref, incoming_ref, received_ref):
    _, half, lanes = incoming_ref.shape
    n = lanes // 2
    left = lax.broadcasted_iota(jnp.int32, (half, lanes), 1) < n
    for slot in range(slots):
        place = partner_ref[slot]
        chunk = jnp.where(place >= 0, incoming_ref[jnp.maximum(place, 0)], 0.0)
        high = chunk.astype(jnp.bfloat16).astype(jnp.float32)
        low = chunk - high
        top = jnp.where(left, high, pltpu.roll(low, n, 1))
        bottom = jnp.where(left, pltpu.roll(high, n, 1), low)
        base = slot * width
        received_ref[base:base + half, :] = top.astype(jnp.bfloat16)
        received_ref[base + half:base + width, :] = bottom.astype(jnp.bfloat16)


def far(loader, received_ref):
    total = None
    for at, size, factor_high, factor_low in loader.parts():
        left = received_ref[loader.rows(at, size), :]
        term = product(left, factor_high, TN) + product(left, factor_low, TN)
        total = term if total is None else total + term
    n = total.shape[0] // 2
    return total[:n] + total[n:]


def project_kernel(partner_ref, ranks_ref, factors_ref, vectors_ref, outgoing_ref,
                   buffer, semaphore):
    loader = Loader(factors_ref, buffer, semaphore)
    loader.start()
    project(loader.parts(), loader.width, vectors_ref[...], partner_ref, ranks_ref, outgoing_ref)


def far_kernel(partner_ref, factors_ref, incoming_ref, base_ref, out_ref, buffer,
               semaphore, received_ref):
    loader = Loader(factors_ref, buffer, semaphore)
    loader.start()
    unpack(loader.width, factors_ref.shape[0], partner_ref, incoming_ref, received_ref)
    out_ref[...] = base_ref[...] - far(loader, received_ref)


def turn_kernel(weights, partner_ref, ranks_ref, factors_ref, incoming_ref,
                base_ref, previous_ref, residual_ref, direction_ref, outgoing_ref, buffer,
                semaphore, received_ref, high_ref, low_ref):
    loader = Loader(factors_ref, buffer, semaphore, high_ref, low_ref)
    loader.start()
    unpack(loader.width, factors_ref.shape[0], partner_ref, incoming_ref, received_ref)
    residual = base_ref[...] - far(loader, received_ref)
    residual_ref[...] = residual
    old, new = weights
    direction = new * residual if old is None else old * previous_ref[...] + new * residual
    direction_ref[...] = direction
    project(loader.kept(), loader.width, direction, partner_ref, ranks_ref, outgoing_ref)


SMEM_SPEC = pl.BlockSpec(memory_space=pltpu.SMEM)
VMEM_SPEC = pl.BlockSpec(memory_space=pltpu.VMEM)
ANY_SPEC = pl.BlockSpec(memory_space=pltpu.HBM)


def body(right_side, start, diag_tiles, neighbour_tiles, factors, partner, ranks):
    device_count = lax.axis_size(AXES)
    right_side, start = right_side[0], start[0]
    diag_block, neighbour_block, factor_block = diag_tiles[0], neighbour_tiles[0], factors[0]
    partner, ranks = partner[0], ranks[0]
    factor_block = pltpu.with_memory_space_constraint(factor_block, pltpu.HBM)
    slots, rank_width, points = factor_block.shape
    n = start.shape[0]
    rows = slots * rank_width
    block = jax.ShapeDtypeStruct((n, points), jnp.float32)
    chunks = jax.ShapeDtypeStruct((device_count, rank_width // 2, 2 * n), jnp.float32)
    loading = [
        pltpu.VMEM((slots, rank_width, points), jnp.float32),
        pltpu.SemaphoreType.DMA((STEPS,)),
    ]
    received = pltpu.VMEM((rows, 2 * n), jnp.bfloat16)
    split = [pltpu.VMEM((rows, points), jnp.bfloat16)] * 2
    params = pltpu.CompilerParams(vmem_limit_bytes=VMEM_LIMIT)

    def cost(times):
        return pl.CostEstimate(
            flops=times * 8 * rows * points * n, bytes_accessed=4 * rows * points,
            transcendentals=0,
        )

    def projected(vectors):
        return pl.pallas_call(
            project_kernel,
            out_shape=chunks,
            in_specs=[SMEM_SPEC, SMEM_SPEC, ANY_SPEC, VMEM_SPEC],
            out_specs=VMEM_SPEC,
            scratch_shapes=loading,
            compiler_params=params,
            cost_estimate=cost(1),
            name="project",
        )(partner, ranks, factor_block, vectors)

    def without_far(incoming, base):
        return pl.pallas_call(
            far_kernel,
            out_shape=block,
            in_specs=[SMEM_SPEC, ANY_SPEC, VMEM_SPEC, VMEM_SPEC],
            out_specs=VMEM_SPEC,
            scratch_shapes=loading + [received],
            compiler_params=params,
            cost_estimate=cost(1),
            name="far",
        )(partner, factor_block, incoming, base)

    def turn(weights, incoming, base, previous):
        return pl.pallas_call(
            functools.partial(turn_kernel, weights),
            out_shape=(block, block, chunks),
            in_specs=[SMEM_SPEC, SMEM_SPEC, ANY_SPEC] + [VMEM_SPEC] * 3,
            out_specs=(VMEM_SPEC,) * 3,
            scratch_shapes=loading + [received] + split,
            compiler_params=params,
            cost_estimate=cost(2),
            name="turn",
        )(partner, ranks, factor_block, incoming, base, previous)

    def finish(outgoing, vectors, before, weights):
        incoming = lax.all_to_all(outgoing, AXES, split_axis=0, concat_axis=0, tiled=True)
        exact = lax.Precision.HIGH
        following = from_behind(vectors, -1)
        carried = lax.dot_general(vectors, neighbour_block, NN, precision=exact)
        lower_term = from_behind(carried, 1)
        local_term = lax.dot_general(vectors, diag_block, NT, precision=exact)
        upper_term = lax.dot_general(following, neighbour_block, NT, precision=exact)
        base = before - (local_term + upper_term + lower_term)
        if weights is None:
            return without_far(incoming, base)
        return turn(weights, incoming, base, vectors)

    center = (spectrum_low + spectrum_high) / 2.0
    half_width = (spectrum_high - spectrum_low) / 2.0
    ratio = center / half_width
    rho_now = 1.0 / ratio
    solution = start
    outgoing = projected(start)
    residual, direction, outgoing = finish(outgoing, start, right_side, (None, 1.0 / center))
    for iteration in range(ITERS):
        solution = solution + direction
        if iteration + 1 < ITERS:
            rho_next = 1.0 / (2.0 * ratio - rho_now)
            weights = (rho_next * rho_now, 2.0 * rho_next / half_width)
            residual, direction, outgoing = finish(outgoing, direction, residual, weights)
            rho_now = rho_next
        else:
            residual = finish(outgoing, direction, residual, None)
    return (solution[None], residual[None])


def solution(mesh):
    return jax.shard_map(
        body,
        mesh=mesh,
        in_specs=(
            P(AXES, None, None),
            P(AXES, None, None),
            P(AXES, None, None),
            P(AXES, None, None),
            P(AXES, None, None, None),
            P(AXES, None),
            P(AXES, None),
        ),
        out_specs=(P(AXES, None, None), P(AXES, None, None)),
        check_vma=False,
    )
```

```python
import functools

import jax
import jax.numpy as jnp
from jax import lax
from jax.experimental import pallas as pl
from jax.experimental.pallas import tpu as pltpu
from jax.sharding import PartitionSpec as P


ITERS = 2

spectrum_low = 0.7
spectrum_high = 3.6

AXES = ("chain", "grp")
NT = (((1,), (1,)), ((), ()))
NN = (((1,), (0,)), ((), ()))
TN = (((0,), (0,)), ((), ()))
VMEM_LIMIT = 40 * 1024 * 1024


def from_behind(block, distance):
    devices = range(lax.axis_size(AXES))
    route = [(i - distance, i) for i in devices if i - distance in devices]
    return lax.ppermute(block, AXES, route)


def halves(value):
    high = value.astype(jnp.bfloat16)
    low = (value - high.astype(jnp.float32)).astype(jnp.bfloat16)
    return high, low


def product(left, right, form):
    return lax.dot_general(left, right, form, preferred_element_type=jnp.float32)


class Columns:
    def __init__(self, count, factors_ref, buffer, semaphore, high_ref, low_ref):
        self.count, self.factors_ref, self.buffer = count, factors_ref, buffer
        self.semaphore, self.high_ref, self.low_ref = semaphore, high_ref, low_ref
        self.slots, self.width, points = factors_ref.shape
        self.size = points // count

    def block(self, index):
        return pl.ds(pl.multiple_of(index * self.size, self.size), self.size)

    def copy(self, index):
        block = self.block(index)
        return pltpu.make_async_copy(
            self.factors_ref.at[:, :, block], self.buffer.at[:, :, block],
            self.semaphore.at[index],
        )

    def start(self):
        for index in range(self.count):
            self.copy(index).start()

    def load(self, index):
        self.copy(index).wait()
        block = self.block(index)
        values = self.buffer[:, :, block].reshape(self.slots * self.width, self.size)
        self.high_ref[:, block], self.low_ref[:, block] = halves(values)

    def far(self, index, turned_ref):
        block, received = self.block(index), turned_ref[...]
        total = (
            product(received, self.high_ref[:, block], NN)
            + product(received, self.low_ref[:, block], NN)
        )
        n = total.shape[0] // 2
        return total[:n] + total[n:]

    def project(self, index, vectors, sums_ref):
        block = self.block(index)
        operand = jnp.concatenate(halves(vectors), axis=0)
        sums_ref[...] += (
            product(self.high_ref[:, block], operand, NT)
            + product(self.low_ref[:, block], operand, NT)
        )


def each_slot(slots, visit):
    together = next(size for size in (7, 4, 2, 1) if slots % size == 0)

    @pl.loop(0, slots // together)
    def _(group):
        for inner in range(together):
            visit(group * together + inner)


def store_chunks(width, sums_ref, partner_ref, ranks_ref, outgoing_ref):
    rows, lanes = sums_ref.shape
    half = width // 2
    own = lax.axis_index(AXES)
    left = lax.broadcasted_iota(jnp.int32, (half, lanes), 1) < lanes // 2
    rank_index = lax.broadcasted_iota(jnp.int32, (half, lanes), 0) + jnp.where(left, 0, half)

    def visit(slot):
        base = pl.multiple_of(slot * width, 16)
        top = sums_ref[pl.ds(base, half), :]
        bottom = sums_ref[pl.ds(base + half, half), :]
        top = top + pltpu.roll(top, lanes // 2, 1)
        bottom = bottom + pltpu.roll(bottom, lanes // 2, 1)
        chunk = jnp.where(rank_index < ranks_ref[slot], jnp.where(left, top, bottom), 0.0)
        place = partner_ref[slot]
        outgoing_ref[jnp.where(place >= 0, place, own)] = chunk

    each_slot(rows // width, visit)


def unpack(width, slots, partner_ref, incoming_ref, received_ref):
    _, half, lanes = incoming_ref.shape
    n = lanes // 2
    left = lax.broadcasted_iota(jnp.int32, (half, lanes), 1) < n

    def visit(slot):
        place = partner_ref[slot]
        chunk = jnp.where(place >= 0, incoming_ref[jnp.maximum(place, 0)], 0.0)
        high = chunk.astype(jnp.bfloat16).astype(jnp.float32)
        low = chunk - high
        top = jnp.where(left, high, pltpu.roll(low, n, 1))
        bottom = jnp.where(left, pltpu.roll(high, n, 1), low)
        base = pl.multiple_of(slot * width, 16)
        received_ref[pl.ds(base, half), :] = top.astype(jnp.bfloat16)
        received_ref[pl.ds(base + half, half), :] = bottom.astype(jnp.bfloat16)

    each_slot(slots, visit)


def project_kernel(partner_hbm, ranks_hbm, vectors_hbm, factors_ref, outgoing_ref,
                   buffer, semaphore, high_ref, low_ref, sums_ref, partner_ref, ranks_ref,
                   vectors_ref, small_semaphore):
    small = [
        pltpu.make_async_copy(source, target, small_semaphore.at[index])
        for index, (source, target) in enumerate((
            (vectors_hbm, vectors_ref), (partner_hbm, partner_ref), (ranks_hbm, ranks_ref)
        ))
    ]
    for copy in small:
        copy.start()
    columns = Columns(4, factors_ref, buffer, semaphore, high_ref, low_ref)
    columns.start()
    sums_ref[...] = jnp.zeros_like(sums_ref)
    for copy in small:
        copy.wait()

    @pl.loop(0, columns.count)
    def _(index):
        columns.load(index)
        columns.project(index, vectors_ref[:, columns.block(index)], sums_ref)

    store_chunks(columns.width, sums_ref, partner_ref, ranks_ref, outgoing_ref)


def turn_kernel(weights, partner_ref, ranks_ref, factors_ref, incoming_ref, base_ref,
                previous_ref, *rest):
    if weights is None:
        residual_ref, *rest = rest
        buffer, semaphore, high_ref, low_ref, received_ref, turned_ref = rest
    else:
        residual_ref, direction_ref, outgoing_ref, *rest = rest
        buffer, semaphore, high_ref, low_ref, received_ref, turned_ref, sums_ref = rest
    count = 4 if weights is None else 2
    columns = Columns(count, factors_ref, buffer, semaphore, high_ref, low_ref)
    columns.start()
    unpack(columns.width, columns.slots, partner_ref, incoming_ref, received_ref)
    turned_ref[...] = received_ref[...].T
    if weights is not None:
        sums_ref[...] = jnp.zeros_like(sums_ref)

    @pl.loop(0, columns.count)
    def _(index):
        columns.load(index)
        block = columns.block(index)
        residual = base_ref[:, block] - columns.far(index, turned_ref)
        residual_ref[:, block] = residual
        if weights is not None:
            old, new = weights
            direction = new * residual
            if old is not None:
                direction = old * previous_ref[:, block] + direction
            direction_ref[:, block] = direction
            columns.project(index, direction, sums_ref)

    if weights is not None:
        store_chunks(columns.width, sums_ref, partner_ref, ranks_ref, outgoing_ref)


SMEM_SPEC = pl.BlockSpec(memory_space=pltpu.SMEM)
VMEM_SPEC = pl.BlockSpec(memory_space=pltpu.VMEM)
ANY_SPEC = pl.BlockSpec(memory_space=pltpu.HBM)


def body(right_side, start, diag_tiles, neighbour_tiles, factors, partner, ranks):
    device_count = lax.axis_size(AXES)
    right_side, start = right_side[0], start[0]
    diag_block, neighbour_block, factor_block = diag_tiles[0], neighbour_tiles[0], factors[0]
    partner, ranks = partner[0], ranks[0]
    factor_block = pltpu.with_memory_space_constraint(factor_block, pltpu.HBM)
    slots, rank_width, points = factor_block.shape
    n = start.shape[0]
    rows = slots * rank_width
    block = jax.ShapeDtypeStruct((n, points), jnp.float32)
    chunks = jax.ShapeDtypeStruct((device_count, rank_width // 2, 2 * n), jnp.float32)
    loading = [
        pltpu.VMEM((slots, rank_width, points), jnp.float32),
        pltpu.SemaphoreType.DMA((4,)),
        pltpu.VMEM((rows, points), jnp.bfloat16),
        pltpu.VMEM((rows, points), jnp.bfloat16),
    ]
    received = [
        pltpu.VMEM((rows, 2 * n), jnp.bfloat16),
        pltpu.VMEM((2 * n, rows), jnp.bfloat16),
    ]
    sums = pltpu.VMEM((rows, 2 * n), jnp.float32)
    params = pltpu.CompilerParams(vmem_limit_bytes=VMEM_LIMIT)

    def cost(times):
        return pl.CostEstimate(
            flops=times * 8 * rows * points * n, bytes_accessed=4 * rows * points,
            transcendentals=0,
        )

    def in_place(array):
        return pltpu.with_memory_space_constraint(array, pltpu.HBM)

    def projected(vectors):
        return pl.pallas_call(
            project_kernel,
            out_shape=chunks,
            in_specs=[ANY_SPEC] * 4,
            out_specs=VMEM_SPEC,
            scratch_shapes=loading + [
                sums,
                pltpu.SMEM((slots,), jnp.int32),
                pltpu.SMEM((slots,), jnp.int32),
                pltpu.VMEM((n, points), jnp.float32),
                pltpu.SemaphoreType.DMA((3,)),
            ],
            compiler_params=params,
            cost_estimate=cost(1),
            name="project",
        )(in_place(partner), in_place(ranks), in_place(vectors), factor_block)

    def turn(weights, incoming, base, previous):
        last = weights is None
        outs = (block,) if last else (block, block, chunks)
        return pl.pallas_call(
            functools.partial(turn_kernel, weights),
            out_shape=outs,
            in_specs=[SMEM_SPEC, SMEM_SPEC, ANY_SPEC] + [VMEM_SPEC] * 3,
            out_specs=(VMEM_SPEC,) * len(outs),
            scratch_shapes=loading + received + ([] if last else [sums]),
            compiler_params=params,
            cost_estimate=cost(1 if last else 2),
            name="far" if last else "turn",
        )(partner, ranks, factor_block, incoming, base, previous)

    def finish(outgoing, vectors, before, weights):
        incoming = lax.all_to_all(outgoing, AXES, split_axis=0, concat_axis=0, tiled=True)
        exact = lax.Precision.HIGH
        following = from_behind(vectors, -1)
        carried = lax.dot_general(vectors, neighbour_block, NN, precision=exact)
        lower_term = from_behind(carried, 1)
        local_term = lax.dot_general(vectors, diag_block, NT, precision=exact)
        upper_term = lax.dot_general(following, neighbour_block, NT, precision=exact)
        base = before - (local_term + upper_term + lower_term)
        return turn(weights, incoming, base, vectors)

    center = (spectrum_low + spectrum_high) / 2.0
    half_width = (spectrum_high - spectrum_low) / 2.0
    ratio = center / half_width
    rho_now = 1.0 / ratio
    solution = start
    outgoing = projected(start)
    residual, direction, outgoing = finish(outgoing, start, right_side, (None, 1.0 / center))
    for iteration in range(ITERS):
        solution = solution + direction
        if iteration + 1 < ITERS:
            rho_next = 1.0 / (2.0 * ratio - rho_now)
            weights = (rho_next * rho_now, 2.0 * rho_next / half_width)
            residual, direction, outgoing = finish(outgoing, direction, residual, weights)
            rho_now = rho_next
        else:
            (residual,) = finish(outgoing, direction, residual, None)
    return (solution[None], residual[None])


def solution(mesh):
    return jax.shard_map(
        body,
        mesh=mesh,
        in_specs=(
            P(AXES, None, None),
            P(AXES, None, None),
            P(AXES, None, None),
            P(AXES, None, None),
            P(AXES, None, None, None),
            P(AXES, None),
            P(AXES, None),
        ),
        out_specs=(P(AXES, None, None), P(AXES, None, None)),
        check_vma=False,
    )
```

```python
import functools

import jax
import jax.numpy as jnp
from jax import lax
from jax.experimental import pallas as pl
from jax.experimental.pallas import tpu as pltpu
from jax.sharding import PartitionSpec as P


ITERS = 2

spectrum_low = 0.7
spectrum_high = 3.6

AXES = ("chain", "grp")
NT = (((1,), (1,)), ((), ()))
NN = (((1,), (0,)), ((), ()))
TN = (((0,), (0,)), ((), ()))
VMEM_LIMIT = 40 * 1024 * 1024


def from_behind(block, distance):
    devices = range(lax.axis_size(AXES))
    route = [(i - distance, i) for i in devices if i - distance in devices]
    return lax.ppermute(block, AXES, route)


def halves(value):
    high = value.astype(jnp.bfloat16)
    low = (value - high.astype(jnp.float32)).astype(jnp.bfloat16)
    return high, low


def product(left, right, form):
    return lax.dot_general(left, right, form, preferred_element_type=jnp.float32)


class Columns:
    def __init__(self, factors_ref, buffer, semaphore, split_ref):
        self.factors_ref, self.buffer = factors_ref, buffer
        self.semaphore, self.split_ref = semaphore, split_ref
        self.count, self.slots, self.width, self.size = buffer.shape

    def block(self, index):
        return pl.ds(pl.multiple_of(index * self.size, self.size), self.size)

    def copy(self, index):
        return pltpu.make_async_copy(
            self.factors_ref.at[:, :, self.block(index)], self.buffer.at[index],
            self.semaphore.at[index],
        )

    def start(self):
        for index in range(self.count):
            self.copy(index).start()

    def load(self, index):
        self.copy(index).wait()
        values = self.buffer[index].reshape(self.slots * self.width, self.size)
        self.split_ref[:, :self.size], self.split_ref[:, self.size:] = halves(values)

    def far(self, turned_ref):
        total = product(turned_ref[...], self.split_ref[...], NN)
        n = total.shape[0] // 2
        total = total[:n] + total[n:]
        return total[:, :self.size] + total[:, self.size:]

    def project(self, vectors, sums_ref):
        operand = jnp.concatenate(halves(vectors), axis=0)
        operand = jnp.concatenate([operand, operand], axis=1)
        sums_ref[...] += product(self.split_ref[...], operand, NT)


def each_slot(slots, visit):
    together = next(size for size in (7, 4, 2, 1) if slots % size == 0)

    @pl.loop(0, slots // together)
    def _(group):
        for inner in range(together):
            visit(group * together + inner)


def store_chunks(width, sums_ref, partner_ref, ranks_ref, outgoing_ref):
    rows, lanes = sums_ref.shape
    half = width // 2
    own = lax.axis_index(AXES)
    left = lax.broadcasted_iota(jnp.int32, (half, lanes), 1) < lanes // 2
    rank_index = lax.broadcasted_iota(jnp.int32, (half, lanes), 0) + jnp.where(left, 0, half)

    def visit(slot):
        base = pl.multiple_of(slot * width, 16)
        top = sums_ref[pl.ds(base, half), :]
        bottom = sums_ref[pl.ds(base + half, half), :]
        top = top + pltpu.roll(top, lanes // 2, 1)
        bottom = bottom + pltpu.roll(bottom, lanes // 2, 1)
        chunk = jnp.where(rank_index < ranks_ref[slot], jnp.where(left, top, bottom), 0.0)
        place = partner_ref[slot]
        outgoing_ref[jnp.where(place >= 0, place, own)] = chunk

    each_slot(rows // width, visit)


def unpack(width, slots, partner_ref, incoming_ref, received_ref):
    _, half, lanes = incoming_ref.shape
    n = lanes // 2
    left = lax.broadcasted_iota(jnp.int32, (half, lanes), 1) < n

    def visit(slot):
        place = partner_ref[slot]
        chunk = jnp.where(place >= 0, incoming_ref[jnp.maximum(place, 0)], 0.0)
        high = chunk.astype(jnp.bfloat16).astype(jnp.float32)
        low = chunk - high
        top = jnp.where(left, high, pltpu.roll(low, n, 1))
        bottom = jnp.where(left, pltpu.roll(high, n, 1), low)
        base = pl.multiple_of(slot * width, 16)
        received_ref[pl.ds(base, half), :] = top.astype(jnp.bfloat16)
        received_ref[pl.ds(base + half, half), :] = bottom.astype(jnp.bfloat16)

    each_slot(slots, visit)


def project_kernel(partner_hbm, ranks_hbm, vectors_hbm, factors_ref, outgoing_ref,
                   buffer, semaphore, split_ref, sums_ref, partner_ref, ranks_ref,
                   vectors_ref, small_semaphore):
    small = [
        pltpu.make_async_copy(source, target, small_semaphore.at[index])
        for index, (source, target) in enumerate((
            (vectors_hbm, vectors_ref), (partner_hbm, partner_ref), (ranks_hbm, ranks_ref)
        ))
    ]
    for copy in small:
        copy.start()
    columns = Columns(factors_ref, buffer, semaphore, split_ref)
    columns.start()
    sums_ref[...] = jnp.zeros_like(sums_ref)
    for copy in small:
        copy.wait()

    @pl.loop(0, columns.count)
    def _(index):
        columns.load(index)
        columns.project(vectors_ref[:, columns.block(index)], sums_ref)

    store_chunks(columns.width, sums_ref, partner_ref, ranks_ref, outgoing_ref)


def turn_kernel(weights, partner_ref, ranks_ref, factors_ref, incoming_ref, base_ref,
                previous_ref, *rest):
    if weights is None:
        residual_ref, *rest = rest
        buffer, semaphore, split_ref, received_ref, turned_ref = rest
    else:
        residual_ref, direction_ref, outgoing_ref, *rest = rest
        buffer, semaphore, split_ref, received_ref, turned_ref, sums_ref = rest
    columns = Columns(factors_ref, buffer, semaphore, split_ref)
    columns.start()
    unpack(columns.width, columns.slots, partner_ref, incoming_ref, received_ref)
    turned_ref[...] = received_ref[...].T
    if weights is not None:
        sums_ref[...] = jnp.zeros_like(sums_ref)

    @pl.loop(0, columns.count)
    def _(index):
        columns.load(index)
        block = columns.block(index)
        residual = base_ref[:, block] - columns.far(turned_ref)
        residual_ref[:, block] = residual
        if weights is not None:
            old, new = weights
            direction = new * residual
            if old is not None:
                direction = old * previous_ref[:, block] + direction
            direction_ref[:, block] = direction
            columns.project(direction, sums_ref)

    if weights is not None:
        store_chunks(columns.width, sums_ref, partner_ref, ranks_ref, outgoing_ref)


SMEM_SPEC = pl.BlockSpec(memory_space=pltpu.SMEM)
VMEM_SPEC = pl.BlockSpec(memory_space=pltpu.VMEM)
ANY_SPEC = pl.BlockSpec(memory_space=pltpu.HBM)


def body(right_side, start, diag_tiles, neighbour_tiles, factors, partner, ranks):
    device_count = lax.axis_size(AXES)
    right_side, start = right_side[0], start[0]
    diag_block, neighbour_block, factor_block = diag_tiles[0], neighbour_tiles[0], factors[0]
    partner, ranks = partner[0], ranks[0]
    factor_block = pltpu.with_memory_space_constraint(factor_block, pltpu.HBM)
    slots, rank_width, points = factor_block.shape
    n = start.shape[0]
    rows = slots * rank_width
    block = jax.ShapeDtypeStruct((n, points), jnp.float32)
    chunks = jax.ShapeDtypeStruct((device_count, rank_width // 2, 2 * n), jnp.float32)
    def loading(blocks):
        return [
            pltpu.VMEM((blocks, slots, rank_width, points // blocks), jnp.float32),
            pltpu.SemaphoreType.DMA((blocks,)),
            pltpu.VMEM((rows, 2 * points // blocks), jnp.bfloat16),
        ]

    received = [
        pltpu.VMEM((rows, 2 * n), jnp.bfloat16),
        pltpu.VMEM((2 * n, rows), jnp.bfloat16),
    ]
    sums = pltpu.VMEM((rows, 2 * n), jnp.float32)
    params = pltpu.CompilerParams(vmem_limit_bytes=VMEM_LIMIT)

    def cost(times):
        return pl.CostEstimate(
            flops=times * 8 * rows * points * n, bytes_accessed=4 * rows * points,
            transcendentals=0,
        )

    def in_place(array):
        return pltpu.with_memory_space_constraint(array, pltpu.HBM)

    def projected(vectors):
        return pl.pallas_call(
            project_kernel,
            out_shape=chunks,
            in_specs=[ANY_SPEC] * 4,
            out_specs=VMEM_SPEC,
            scratch_shapes=loading(4) + [
                sums,
                pltpu.SMEM((slots,), jnp.int32),
                pltpu.SMEM((slots,), jnp.int32),
                pltpu.VMEM((n, points), jnp.float32),
                pltpu.SemaphoreType.DMA((3,)),
            ],
            compiler_params=params,
            cost_estimate=cost(1),
            name="project",
        )(in_place(partner), in_place(ranks), in_place(vectors), factor_block)

    def turn(weights, incoming, base, previous):
        last = weights is None
        outs = (block,) if last else (block, block, chunks)
        return pl.pallas_call(
            functools.partial(turn_kernel, weights),
            out_shape=outs,
            in_specs=[SMEM_SPEC, SMEM_SPEC, ANY_SPEC] + [VMEM_SPEC] * 3,
            out_specs=(VMEM_SPEC,) * len(outs),
            scratch_shapes=loading(4 if last else 2) + received + ([] if last else [sums]),
            compiler_params=params,
            cost_estimate=cost(1 if last else 2),
            name="far" if last else "turn",
        )(partner, ranks, factor_block, incoming, base, previous)

    def finish(outgoing, vectors, before, weights):
        incoming = lax.all_to_all(outgoing, AXES, split_axis=0, concat_axis=0, tiled=True)
        exact = lax.Precision.HIGH
        following = from_behind(vectors, -1)
        carried = lax.dot_general(vectors, neighbour_block, NN, precision=exact)
        lower_term = from_behind(carried, 1)
        partial = before - lax.dot_general(vectors, diag_block, NT, precision=exact)
        partial = lax.optimization_barrier(partial)
        upper_term = lax.dot_general(following, neighbour_block, NT, precision=exact)
        base = partial - (upper_term + lower_term)
        return turn(weights, incoming, base, vectors)

    center = (spectrum_low + spectrum_high) / 2.0
    half_width = (spectrum_high - spectrum_low) / 2.0
    ratio = center / half_width
    rho_now = 1.0 / ratio
    solution = start
    outgoing = projected(start)
    residual, direction, outgoing = finish(outgoing, start, right_side, (None, 1.0 / center))
    for iteration in range(ITERS):
        solution = solution + direction
        if iteration + 1 < ITERS:
            rho_next = 1.0 / (2.0 * ratio - rho_now)
            weights = (rho_next * rho_now, 2.0 * rho_next / half_width)
            residual, direction, outgoing = finish(outgoing, direction, residual, weights)
            rho_now = rho_next
        else:
            (residual,) = finish(outgoing, direction, residual, None)
    return (solution[None], residual[None])


def solution(mesh):
    return jax.shard_map(
        body,
        mesh=mesh,
        in_specs=(
            P(AXES, None, None),
            P(AXES, None, None),
            P(AXES, None, None),
            P(AXES, None, None),
            P(AXES, None, None, None),
            P(AXES, None),
            P(AXES, None),
        ),
        out_specs=(P(AXES, None, None), P(AXES, None, None)),
        check_vma=False,
    )
```

```python
import functools

import jax
import jax.numpy as jnp
from jax import lax
from jax.experimental import pallas as pl
from jax.experimental.pallas import tpu as pltpu
from jax.sharding import PartitionSpec as P


ITERS = 2

spectrum_low = 0.7
spectrum_high = 3.6

AXES = ("chain", "grp")
NT = (((1,), (1,)), ((), ()))
NN = (((1,), (0,)), ((), ()))
TN = (((0,), (0,)), ((), ()))
VMEM_LIMIT = 40 * 1024 * 1024


def from_behind(block, distance):
    devices = range(lax.axis_size(AXES))
    route = [(i - distance, i) for i in devices if i - distance in devices]
    return lax.ppermute(block, AXES, route)


def halves(value):
    high = value.astype(jnp.bfloat16)
    low = (value - high.astype(jnp.float32)).astype(jnp.bfloat16)
    return high, low


def product(left, right, form):
    return lax.dot_general(left, right, form, preferred_element_type=jnp.float32)


def cuts(rows, parts):
    edges = [rows * part // parts // 256 * 256 for part in range(parts)] + [rows]
    return [(first, last) for first, last in zip(edges, edges[1:]) if last > first]


class Pieces:
    def __init__(self, rectangles, factors_ref, buffer, semaphore, split_ref):
        self.rectangles, self.factors_ref, self.buffer = rectangles, factors_ref, buffer
        self.semaphore, self.split_ref = semaphore, split_ref

    def copy(self, index):
        rows, columns = (slice(*edges) for edges in self.rectangles[index])
        return pltpu.make_async_copy(
            self.factors_ref.at[rows, columns], self.buffer.at[rows, columns],
            self.semaphore.at[index],
        )

    def start(self):
        for index in range(len(self.rectangles)):
            self.copy(index).start()

    def load(self, index):
        self.copy(index).wait()
        rows, columns = (slice(*edges) for edges in self.rectangles[index])
        high, low = halves(self.buffer[rows, columns])
        width = high.shape[1]
        self.split_ref[rows, :width], self.split_ref[rows, width:2 * width] = high, low

    def far(self, index, turned_ref):
        (first, last), (left, right) = self.rectangles[index]
        width = right - left
        total = product(turned_ref[:, first:last], self.split_ref[first:last, :2 * width], NN)
        n = total.shape[0] // 2
        total = total[:n] + total[n:]
        return total[:, :width] + total[:, width:]


def operand_of(vectors):
    operand = jnp.concatenate(halves(vectors), axis=0).T
    return jnp.concatenate([operand, operand], axis=0)


def project(split_ref, vectors, sums_ref, first):
    total = product(split_ref[:, :2 * vectors.shape[1]], operand_of(vectors), NN)
    sums_ref[...] = total if first else sums_ref[...] + total


def project_last(split_ref, vectors, sums_ref, width, partner_ref, ranks_ref, outgoing_ref):
    operand = operand_of(vectors)
    rows, lanes = sums_ref.shape
    half = width // 2
    own = lax.axis_index(AXES)
    left = lax.broadcasted_iota(jnp.int32, (half, lanes), 1) < lanes // 2
    rank_index = lax.broadcasted_iota(jnp.int32, (half, lanes), 0) + jnp.where(left, 0, half)
    slots = rows // width
    together = -(-slots // 4)
    for at in range(0, slots, together):
        end = min(at + together, slots)
        some = slice(at * width, end * width)
        total = sums_ref[some, :] + product(split_ref[some, :operand.shape[0]], operand, NN)
        total = total + pltpu.roll(total, lanes // 2, 1)
        for slot in range(at, end):
            base = (slot - at) * width
            chunk = jnp.where(left, total[base:base + half], total[base + half:base + width])
            chunk = jnp.where(rank_index < ranks_ref[slot], chunk, 0.0)
            place = partner_ref[slot]
            outgoing_ref[jnp.where(place >= 0, place, own)] = chunk


def apart(partner_ref):
    return pl.when(partner_ref[0] >= -1)


def each_slot(slots, visit):
    together = next(size for size in (7, 4, 2, 1) if slots % size == 0)

    @pl.loop(0, slots // together)
    def _(group):
        for inner in range(together):
            visit(group * together + inner)


def unpack(width, slots, partner_ref, incoming_ref, received_ref):
    _, half, lanes = incoming_ref.shape
    n = lanes // 2
    left = lax.broadcasted_iota(jnp.int32, (half, lanes), 1) < n

    def visit(slot):
        place = partner_ref[slot]
        chunk = jnp.where(place >= 0, incoming_ref[jnp.maximum(place, 0)], 0.0)
        high = chunk.astype(jnp.bfloat16).astype(jnp.float32)
        low = chunk - high
        top = jnp.where(left, high, pltpu.roll(low, n, 1))
        bottom = jnp.where(left, pltpu.roll(high, n, 1), low)
        base = pl.multiple_of(slot * width, 16)
        received_ref[pl.ds(base, half), :] = top.astype(jnp.bfloat16)
        received_ref[pl.ds(base + half, half), :] = bottom.astype(jnp.bfloat16)

    each_slot(slots, visit)


def project_kernel(rectangles, width, partner_hbm, ranks_hbm, vectors_hbm, factors_ref,
                   outgoing_ref, buffer, semaphore, split_ref, sums_ref, partner_ref, ranks_ref,
                   vectors_ref, small_semaphore):
    small = [
        pltpu.make_async_copy(source, target, small_semaphore.at[index])
        for index, (source, target) in enumerate((
            (vectors_hbm, vectors_ref), (partner_hbm, partner_ref), (ranks_hbm, ranks_ref)
        ))
    ]
    for copy in small:
        copy.start()
    pieces = Pieces(rectangles, factors_ref, buffer, semaphore, split_ref)
    pieces.start()
    for copy in small:
        copy.wait()
    for index, (_, columns) in enumerate(rectangles):
        @apart(partner_ref)
        def _():
            pieces.load(index)
            vectors = vectors_ref[:, slice(*columns)]
            if index + 1 < len(rectangles):
                project(split_ref, vectors, sums_ref, index == 0)
            else:
                project_last(
                    split_ref, vectors, sums_ref, width, partner_ref, ranks_ref, outgoing_ref
                )


def turn_kernel(weights, rectangles, width, partner_ref, ranks_ref, factors_ref, incoming_ref,
                base_ref, previous_ref, *rest):
    if weights is None:
        residual_ref, *rest = rest
        buffer, semaphore, split_ref, received_ref, turned_ref = rest
    else:
        residual_ref, direction_ref, outgoing_ref, *rest = rest
        buffer, semaphore, split_ref, received_ref, turned_ref, sums_ref = rest
    pieces = Pieces(rectangles, factors_ref, buffer, semaphore, split_ref)
    pieces.start()
    unpack(width, factors_ref.shape[0] // width, partner_ref, incoming_ref, received_ref)
    turned_ref[...] = received_ref[...].T
    rows = factors_ref.shape[0]
    for index, ((first, last), columns) in enumerate(rectangles):
        @apart(partner_ref)
        def _():
            block = slice(*columns)
            pieces.load(index)
            before = base_ref if first == 0 else residual_ref
            residual = before[:, block] - pieces.far(index, turned_ref)
            residual_ref[:, block] = residual
            if weights is None or last < rows:
                return
            old, new = weights
            direction = new * residual
            if old is not None:
                direction = old * previous_ref[:, block] + direction
            direction_ref[:, block] = direction
            if index + 1 < len(rectangles):
                project(split_ref, direction, sums_ref, columns[0] == 0)
            else:
                project_last(
                    split_ref, direction, sums_ref, width, partner_ref, ranks_ref, outgoing_ref
                )


SMEM_SPEC = pl.BlockSpec(memory_space=pltpu.SMEM)
VMEM_SPEC = pl.BlockSpec(memory_space=pltpu.VMEM)
ANY_SPEC = pl.BlockSpec(memory_space=pltpu.HBM)


def body(right_side, start, diag_tiles, neighbour_tiles, factors, partner, ranks):
    device_count = lax.axis_size(AXES)
    right_side, start = right_side[0], start[0]
    diag_block, neighbour_block, factor_block = diag_tiles[0], neighbour_tiles[0], factors[0]
    partner, ranks = partner[0], ranks[0]
    slots, rank_width, points = factor_block.shape
    n = start.shape[0]
    rows = slots * rank_width
    block = jax.ShapeDtypeStruct((n, points), jnp.float32)
    chunks = jax.ShapeDtypeStruct((device_count, rank_width // 2, 2 * n), jnp.float32)
    factor_block = factor_block.reshape(rows, points)
    factor_block = pltpu.with_memory_space_constraint(factor_block, pltpu.HBM)
    middle, quarter = points // 2, points // 4
    by_columns = [((0, rows), (at, at + quarter)) for at in range(0, points, quarter)]
    by_halves = [(part, (0, middle)) for part in cuts(rows, 2)] + [((0, rows), (middle, points))]

    def loading(rectangles):
        width = max(right - left for _, (left, right) in rectangles)
        return [
            pltpu.VMEM((rows, points), jnp.float32),
            pltpu.SemaphoreType.DMA((len(rectangles),)),
            pltpu.VMEM((rows, 2 * width), jnp.bfloat16),
        ]

    received = [
        pltpu.VMEM((rows, 2 * n), jnp.bfloat16),
        pltpu.VMEM((2 * n, rows), jnp.bfloat16),
    ]
    sums = pltpu.VMEM((rows, 2 * n), jnp.float32)
    params = pltpu.CompilerParams(vmem_limit_bytes=VMEM_LIMIT)

    def cost(times):
        return pl.CostEstimate(
            flops=times * 8 * rows * points * n, bytes_accessed=4 * rows * points,
            transcendentals=0,
        )

    def in_place(array):
        return pltpu.with_memory_space_constraint(array, pltpu.HBM)

    def projected(vectors):
        return pl.pallas_call(
            functools.partial(project_kernel, by_columns, rank_width),
            out_shape=chunks,
            in_specs=[ANY_SPEC] * 4,
            out_specs=VMEM_SPEC,
            scratch_shapes=loading(by_columns) + [
                sums,
                pltpu.SMEM((slots,), jnp.int32),
                pltpu.SMEM((slots,), jnp.int32),
                pltpu.VMEM((n, points), jnp.float32),
                pltpu.SemaphoreType.DMA((3,)),
            ],
            compiler_params=params,
            cost_estimate=cost(1),
            name="project",
        )(in_place(partner), in_place(ranks), in_place(vectors), factor_block)

    def turn(weights, incoming, base, previous):
        last = weights is None
        rectangles = by_columns if last else by_halves
        outs = (block,) if last else (block, block, chunks)
        return pl.pallas_call(
            functools.partial(turn_kernel, weights, rectangles, rank_width),
            out_shape=outs,
            in_specs=[SMEM_SPEC, SMEM_SPEC, ANY_SPEC] + [VMEM_SPEC] * 3,
            out_specs=(VMEM_SPEC,) * len(outs),
            scratch_shapes=loading(rectangles) + received + ([] if last else [sums]),
            compiler_params=params,
            cost_estimate=cost(1 if last else 2),
            name="far" if last else "turn",
        )(partner, ranks, factor_block, incoming, base, previous)

    def finish(outgoing, vectors, before, weights):
        incoming = lax.all_to_all(outgoing, AXES, split_axis=0, concat_axis=0, tiled=True)
        exact = lax.Precision.HIGH
        following = from_behind(vectors, -1)
        carried = lax.dot_general(vectors, neighbour_block, NN, precision=exact)
        lower_term = from_behind(carried, 1)
        partial = before - lax.dot_general(vectors, diag_block, NT, precision=exact)
        partial = lax.optimization_barrier(partial)
        upper_term = lax.dot_general(following, neighbour_block, NT, precision=exact)
        base = partial - (upper_term + lower_term)
        return turn(weights, incoming, base, vectors)

    center = (spectrum_low + spectrum_high) / 2.0
    half_width = (spectrum_high - spectrum_low) / 2.0
    ratio = center / half_width
    rho_now = 1.0 / ratio
    solution = start
    outgoing = projected(start)
    residual, direction, outgoing = finish(outgoing, start, right_side, (None, 1.0 / center))
    for iteration in range(ITERS):
        solution = solution + direction
        if iteration + 1 < ITERS:
            rho_next = 1.0 / (2.0 * ratio - rho_now)
            weights = (rho_next * rho_now, 2.0 * rho_next / half_width)
            residual, direction, outgoing = finish(outgoing, direction, residual, weights)
            rho_now = rho_next
        else:
            (residual,) = finish(outgoing, direction, residual, None)
    return (solution[None], residual[None])


def solution(mesh):
    return jax.shard_map(
        body,
        mesh=mesh,
        in_specs=(
            P(AXES, None, None),
            P(AXES, None, None),
            P(AXES, None, None),
            P(AXES, None, None),
            P(AXES, None, None, None),
            P(AXES, None),
            P(AXES, None),
        ),
        out_specs=(P(AXES, None, None), P(AXES, None, None)),
        check_vma=False,
    )
```

```python
import functools

import jax
import jax.numpy as jnp
from jax import lax
from jax.experimental import pallas as pl
from jax.experimental.pallas import tpu as pltpu
from jax.sharding import PartitionSpec as P


ITERS = 2

spectrum_low = 0.7
spectrum_high = 3.6

AXES = ("chain", "grp")
NT = (((1,), (1,)), ((), ()))
NN = (((1,), (0,)), ((), ()))
VMEM_LIMIT = 40 * 1024 * 1024


def from_behind(block, distance):
    devices = range(lax.axis_size(AXES))
    route = [(i - distance, i) for i in devices if i - distance in devices]
    return lax.ppermute(block, AXES, route)


def halves(value):
    high = value.astype(jnp.bfloat16)
    low = (value - high.astype(jnp.float32)).astype(jnp.bfloat16)
    return high, low


def product(left, right, form):
    return lax.dot_general(left, right, form, preferred_element_type=jnp.float32)


def cuts(rows, parts):
    edges = [rows * part // parts // 256 * 256 for part in range(parts)] + [rows]
    return [(first, last) for first, last in zip(edges, edges[1:]) if last > first]


class Pieces:
    def __init__(self, rectangles, factors_ref, buffer, semaphore, split_ref):
        self.rectangles, self.factors_ref, self.buffer = rectangles, factors_ref, buffer
        self.semaphore, self.split_ref = semaphore, split_ref

    def copy(self, index):
        rows, columns = (slice(*edges) for edges in self.rectangles[index])
        return pltpu.make_async_copy(
            self.factors_ref.at[rows, columns], self.buffer.at[rows, columns],
            self.semaphore.at[index],
        )

    def start(self):
        for index in range(len(self.rectangles)):
            self.copy(index).start()

    def load(self, index):
        self.copy(index).wait()
        rows, columns = (slice(*edges) for edges in self.rectangles[index])
        high, low = halves(self.buffer[rows, columns])
        width = high.shape[1]
        self.split_ref[rows, :width], self.split_ref[rows, width:2 * width] = high, low

    def far(self, index, turned_ref):
        (first, last), (left, right) = self.rectangles[index]
        width = right - left
        total = product(turned_ref[:, first:last], self.split_ref[first:last, :2 * width], NN)
        n = total.shape[0] // 2
        total = total[:n] + total[n:]
        return total[:, :width] + total[:, width:]


def operand_of(vectors):
    operand = jnp.concatenate(halves(vectors), axis=0).T
    return jnp.concatenate([operand, operand], axis=0)


def project(split_ref, vectors, sums_ref, first):
    total = product(split_ref[:, :2 * vectors.shape[1]], operand_of(vectors), NN)
    sums_ref[...] = total if first else sums_ref[...] + total


def project_last(split_ref, vectors, sums_ref, width, partner_ref, ranks_ref, outgoing_ref):
    operand = operand_of(vectors)
    rows, lanes = sums_ref.shape
    half = width // 2
    own = lax.axis_index(AXES)
    left = lax.broadcasted_iota(jnp.int32, (half, lanes), 1) < lanes // 2
    rank_index = lax.broadcasted_iota(jnp.int32, (half, lanes), 0) + jnp.where(left, 0, half)
    slots = rows // width
    together = -(-slots // 4)
    for at in range(0, slots, together):
        end = min(at + together, slots)
        some = slice(at * width, end * width)
        total = sums_ref[some, :] + product(split_ref[some, :operand.shape[0]], operand, NN)
        total = total + pltpu.roll(total, lanes // 2, 1)
        for slot in range(at, end):
            base = (slot - at) * width
            chunk = jnp.where(left, total[base:base + half], total[base + half:base + width])
            chunk = jnp.where(rank_index < ranks_ref[slot], chunk, 0.0)
            place = partner_ref[slot]
            outgoing_ref[jnp.where(place >= 0, place, own)] = chunk


def apart(partner_ref):
    return pl.when(partner_ref[0] >= -1)


def each_slot(slots, visit):
    together = next(size for size in (7, 4, 2, 1) if slots % size == 0)

    @pl.loop(0, slots // together)
    def _(group):
        for inner in range(together):
            visit(group * together + inner)


def unpack(width, slots, partner_ref, incoming_ref, received_ref):
    _, half, lanes = incoming_ref.shape
    n = lanes // 2
    left = lax.broadcasted_iota(jnp.int32, (half, lanes), 1) < n

    def visit(slot):
        place = partner_ref[slot]
        chunk = jnp.where(place >= 0, incoming_ref[jnp.maximum(place, 0)], 0.0)
        high = chunk.astype(jnp.bfloat16).astype(jnp.float32)
        low = chunk - high
        top = jnp.where(left, high, pltpu.roll(low, n, 1))
        bottom = jnp.where(left, pltpu.roll(high, n, 1), low)
        base = pl.multiple_of(slot * width, 16)
        received_ref[pl.ds(base, half), :] = top.astype(jnp.bfloat16)
        received_ref[pl.ds(base + half, half), :] = bottom.astype(jnp.bfloat16)

    each_slot(slots, visit)


def project_kernel(rectangles, width, partner_hbm, ranks_hbm, vectors_hbm, factors_ref,
                   outgoing_ref, buffer, semaphore, split_ref, sums_ref, partner_ref, ranks_ref,
                   vectors_ref, small_semaphore):
    small = [
        pltpu.make_async_copy(source, target, small_semaphore.at[index])
        for index, (source, target) in enumerate((
            (vectors_hbm, vectors_ref), (partner_hbm, partner_ref), (ranks_hbm, ranks_ref)
        ))
    ]
    for copy in small:
        copy.start()
    pieces = Pieces(rectangles, factors_ref, buffer, semaphore, split_ref)
    pieces.start()
    for copy in small:
        copy.wait()
    for index, (_, columns) in enumerate(rectangles):
        @apart(partner_ref)
        def _():
            pieces.load(index)
            vectors = vectors_ref[:, slice(*columns)]
            if index + 1 < len(rectangles):
                project(split_ref, vectors, sums_ref, index == 0)
            else:
                project_last(
                    split_ref, vectors, sums_ref, width, partner_ref, ranks_ref, outgoing_ref
                )


def turn_kernel(weights, rectangles, width, partner_ref, ranks_ref, factors_ref, incoming_ref,
                base_ref, lower_ref, previous_ref, *rest):
    if weights is None:
        residual_ref, *rest = rest
        buffer, semaphore, split_ref, received_ref, turned_ref = rest
    else:
        residual_ref, direction_ref, outgoing_ref, *rest = rest
        buffer, semaphore, split_ref, received_ref, turned_ref, sums_ref = rest
    pieces = Pieces(rectangles, factors_ref, buffer, semaphore, split_ref)
    pieces.start()
    unpack(width, factors_ref.shape[0] // width, partner_ref, incoming_ref, received_ref)
    turned_ref[...] = received_ref[...].T
    rows = factors_ref.shape[0]
    for index, ((first, last), columns) in enumerate(rectangles):
        @apart(partner_ref)
        def _():
            block = slice(*columns)
            pieces.load(index)
            if first == 0:
                before = base_ref[:, block] - lower_ref[:, block]
            else:
                before = residual_ref[:, block]
            residual = before - pieces.far(index, turned_ref)
            residual_ref[:, block] = residual
            if weights is None or last < rows:
                return
            old, new = weights
            direction = new * residual
            if old is not None:
                direction = old * previous_ref[:, block] + direction
            direction_ref[:, block] = direction
            if index + 1 < len(rectangles):
                project(split_ref, direction, sums_ref, columns[0] == 0)
            else:
                project_last(
                    split_ref, direction, sums_ref, width, partner_ref, ranks_ref, outgoing_ref
                )


SMEM_SPEC = pl.BlockSpec(memory_space=pltpu.SMEM)
VMEM_SPEC = pl.BlockSpec(memory_space=pltpu.VMEM)
ANY_SPEC = pl.BlockSpec(memory_space=pltpu.HBM)


def body(right_side, start, diag_tiles, neighbour_tiles, factors, partner, ranks):
    device_count = lax.axis_size(AXES)
    right_side, start = right_side[0], start[0]
    diag_block, neighbour_block, factor_block = diag_tiles[0], neighbour_tiles[0], factors[0]
    partner, ranks = partner[0], ranks[0]
    slots, rank_width, points = factor_block.shape
    n = start.shape[0]
    rows = slots * rank_width
    block = jax.ShapeDtypeStruct((n, points), jnp.float32)
    chunks = jax.ShapeDtypeStruct((device_count, rank_width // 2, 2 * n), jnp.float32)
    factor_block = factor_block.reshape(rows, points)
    factor_block = pltpu.with_memory_space_constraint(factor_block, pltpu.HBM)
    middle, quarter = points // 2, points // 4
    by_columns = [((0, rows), (at, at + quarter)) for at in range(0, points, quarter)]
    by_halves = [(part, (0, middle)) for part in cuts(rows, 2)] + [((0, rows), (middle, points))]

    def loading(rectangles):
        width = max(right - left for _, (left, right) in rectangles)
        return [
            pltpu.VMEM((rows, points), jnp.float32),
            pltpu.SemaphoreType.DMA((len(rectangles),)),
            pltpu.VMEM((rows, 2 * width), jnp.bfloat16),
        ]

    received = [
        pltpu.VMEM((rows, 2 * n), jnp.bfloat16),
        pltpu.VMEM((2 * n, rows), jnp.bfloat16),
    ]
    sums = pltpu.VMEM((rows, 2 * n), jnp.float32)
    params = pltpu.CompilerParams(vmem_limit_bytes=VMEM_LIMIT)

    def cost(times):
        return pl.CostEstimate(
            flops=times * 8 * rows * points * n, bytes_accessed=4 * rows * points,
            transcendentals=0,
        )

    def in_place(array):
        return pltpu.with_memory_space_constraint(array, pltpu.HBM)

    def projected(vectors):
        return pl.pallas_call(
            functools.partial(project_kernel, by_columns, rank_width),
            out_shape=chunks,
            in_specs=[ANY_SPEC] * 4,
            out_specs=VMEM_SPEC,
            scratch_shapes=loading(by_columns) + [
                sums,
                pltpu.SMEM((slots,), jnp.int32),
                pltpu.SMEM((slots,), jnp.int32),
                pltpu.VMEM((n, points), jnp.float32),
                pltpu.SemaphoreType.DMA((3,)),
            ],
            compiler_params=params,
            cost_estimate=cost(1),
            name="project",
        )(in_place(partner), in_place(ranks), in_place(vectors), factor_block)

    def turn(weights, incoming, base, lower, previous):
        last = weights is None
        rectangles = by_columns if last else by_halves
        outs = (block,) if last else (block, block, chunks)
        return pl.pallas_call(
            functools.partial(turn_kernel, weights, rectangles, rank_width),
            out_shape=outs,
            in_specs=[SMEM_SPEC, SMEM_SPEC, ANY_SPEC] + [VMEM_SPEC] * 4,
            out_specs=(VMEM_SPEC,) * len(outs),
            scratch_shapes=loading(rectangles) + received + ([] if last else [sums]),
            compiler_params=params,
            cost_estimate=cost(1 if last else 2),
            name="far" if last else "turn",
        )(partner, ranks, factor_block, incoming, base, lower, previous)

    def finish(outgoing, vectors, before, weights):
        exact = lax.Precision.HIGH
        incoming = lax.all_to_all(
            outgoing, AXES, split_axis=0, concat_axis=0, tiled=True
        )
        following = []
        for part in jnp.split(vectors, 2, axis=1):
            following.append(from_behind(part, -1))
        carried = lax.dot_general(vectors, neighbour_block, NN, precision=exact)
        lower_term = from_behind(carried, 1)
        partial = before - lax.dot_general(vectors, diag_block, NT, precision=exact)
        partial = lax.optimization_barrier(partial)
        for part, tile in zip(following, jnp.split(neighbour_block, 2, axis=1)):
            partial = lax.optimization_barrier(
                partial - lax.dot_general(part, tile, NT, precision=exact)
            )
        return turn(weights, incoming, partial, lower_term, vectors)

    center = (spectrum_low + spectrum_high) / 2.0
    half_width = (spectrum_high - spectrum_low) / 2.0
    ratio = center / half_width
    rho_now = 1.0 / ratio
    solution = start
    outgoing = projected(start)
    residual, direction, outgoing = finish(outgoing, start, right_side, (None, 1.0 / center))
    for iteration in range(ITERS):
        solution = solution + direction
        if iteration + 1 < ITERS:
            rho_next = 1.0 / (2.0 * ratio - rho_now)
            weights = (rho_next * rho_now, 2.0 * rho_next / half_width)
            residual, direction, outgoing = finish(outgoing, direction, residual, weights)
            rho_now = rho_next
        else:
            (residual,) = finish(outgoing, direction, residual, None)
    return (solution[None], residual[None])


def solution(mesh):
    return jax.shard_map(
        body,
        mesh=mesh,
        in_specs=(
            P(AXES, None, None),
            P(AXES, None, None),
            P(AXES, None, None),
            P(AXES, None, None),
            P(AXES, None, None, None),
            P(AXES, None),
            P(AXES, None),
        ),
        out_specs=(P(AXES, None, None), P(AXES, None, None)),
        check_vma=False,
    )
```

```python
import functools

import jax
import jax.numpy as jnp
from jax import lax
from jax.experimental import pallas as pl
from jax.experimental.pallas import tpu as pltpu
from jax.sharding import PartitionSpec as P


ITERS = 2

spectrum_low = 0.7
spectrum_high = 3.6

AXES = ("chain", "grp")
NT = (((1,), (1,)), ((), ()))
NN = (((1,), (0,)), ((), ()))
VMEM_LIMIT = 40 * 1024 * 1024


def from_behind(block, distance):
    devices = range(lax.axis_size(AXES))
    route = [(i - distance, i) for i in devices if i - distance in devices]
    return lax.ppermute(block, AXES, route)


def halves(value):
    high = value.astype(jnp.bfloat16)
    low = (value - high.astype(jnp.float32)).astype(jnp.bfloat16)
    return high, low


def product(left, right, form):
    return lax.dot_general(left, right, form, preferred_element_type=jnp.float32)


def cuts(rows, parts):
    edges = [rows * part // parts // 256 * 256 for part in range(parts)] + [rows]
    return [(first, last) for first, last in zip(edges, edges[1:]) if last > first]


class Pieces:
    def __init__(self, rectangles, factors_ref, buffer, semaphore, split_ref, held_ref=None):
        self.rectangles, self.factors_ref, self.buffer = rectangles, factors_ref, buffer
        self.semaphore, self.split_ref, self.held_ref = semaphore, split_ref, held_ref

    def held(self, index):
        return index == 0 and self.held_ref is not None

    def copy(self, index):
        rows, columns = (slice(*edges) for edges in self.rectangles[index])
        return pltpu.make_async_copy(
            self.factors_ref.at[rows, columns], self.buffer.at[rows, columns],
            self.semaphore.at[index],
        )

    def start(self):
        for index in range(len(self.rectangles)):
            if not self.held(index):
                self.copy(index).start()

    def load(self, index):
        rows, columns = (slice(*edges) for edges in self.rectangles[index])
        if self.held(index):
            values = self.held_ref[...]
        else:
            self.copy(index).wait()
            values = self.buffer[rows, columns]
        high, low = halves(values)
        width = high.shape[1]
        self.split_ref[rows, :width], self.split_ref[rows, width:2 * width] = high, low

    def far(self, index, turned_ref):
        (first, last), (left, right) = self.rectangles[index]
        width = right - left
        total = product(turned_ref[:, first:last], self.split_ref[first:last, :2 * width], NN)
        n = total.shape[0] // 2
        total = total[:n] + total[n:]
        return total[:, :width] + total[:, width:]


def operand_of(vectors):
    operand = jnp.concatenate(halves(vectors), axis=0).T
    return jnp.concatenate([operand, operand], axis=0)


def project(split_ref, vectors, sums_ref, first):
    total = product(split_ref[:, :2 * vectors.shape[1]], operand_of(vectors), NN)
    sums_ref[...] = total if first else sums_ref[...] + total


def project_last(split_ref, vectors, sums_ref, width, partner_ref, ranks_ref, outgoing_ref):
    operand = operand_of(vectors)
    rows, lanes = sums_ref.shape
    half = width // 2
    own = lax.axis_index(AXES)
    left = lax.broadcasted_iota(jnp.int32, (half, lanes), 1) < lanes // 2
    rank_index = lax.broadcasted_iota(jnp.int32, (half, lanes), 0) + jnp.where(left, 0, half)
    slots = rows // width
    together = -(-slots // 4)
    for at in range(0, slots, together):
        end = min(at + together, slots)
        some = slice(at * width, end * width)
        total = sums_ref[some, :] + product(split_ref[some, :operand.shape[0]], operand, NN)
        total = total + pltpu.roll(total, lanes // 2, 1)
        for slot in range(at, end):
            base = (slot - at) * width
            chunk = jnp.where(left, total[base:base + half], total[base + half:base + width])
            chunk = jnp.where(rank_index < ranks_ref[slot], chunk, 0.0)
            place = partner_ref[slot]
            outgoing_ref[jnp.where(place >= 0, place, own)] = chunk


def apart(partner_ref):
    return pl.when(partner_ref[0] >= -1)


def each_slot(slots, visit):
    together = next(size for size in (7, 4, 2, 1) if slots % size == 0)

    @pl.loop(0, slots // together)
    def _(group):
        for inner in range(together):
            visit(group * together + inner)


def unpack(width, slots, partner_ref, incoming_ref, received_ref):
    _, half, lanes = incoming_ref.shape
    n = lanes // 2
    left = lax.broadcasted_iota(jnp.int32, (half, lanes), 1) < n

    def visit(slot):
        place = partner_ref[slot]
        chunk = jnp.where(place >= 0, incoming_ref[jnp.maximum(place, 0)], 0.0)
        high = chunk.astype(jnp.bfloat16).astype(jnp.float32)
        low = chunk - high
        top = jnp.where(left, high, pltpu.roll(low, n, 1))
        bottom = jnp.where(left, pltpu.roll(high, n, 1), low)
        base = pl.multiple_of(slot * width, 16)
        received_ref[pl.ds(base, half), :] = top.astype(jnp.bfloat16)
        received_ref[pl.ds(base + half, half), :] = bottom.astype(jnp.bfloat16)

    each_slot(slots, visit)


def project_kernel(rectangles, width, partner_hbm, ranks_hbm, vectors_hbm, factors_ref,
                   outgoing_ref, buffer, semaphore, split_ref, sums_ref, partner_ref, ranks_ref,
                   vectors_ref, small_semaphore):
    small = [
        pltpu.make_async_copy(source, target, small_semaphore.at[index])
        for index, (source, target) in enumerate((
            (vectors_hbm, vectors_ref), (partner_hbm, partner_ref), (ranks_hbm, ranks_ref)
        ))
    ]
    for copy in small:
        copy.start()
    pieces = Pieces(rectangles, factors_ref, buffer, semaphore, split_ref)
    pieces.start()
    for copy in small:
        copy.wait()
    for index, (_, columns) in enumerate(rectangles):
        @apart(partner_ref)
        def _():
            pieces.load(index)
            vectors = vectors_ref[:, slice(*columns)]
            if index + 1 < len(rectangles):
                project(split_ref, vectors, sums_ref, index == 0)
            else:
                project_last(
                    split_ref, vectors, sums_ref, width, partner_ref, ranks_ref, outgoing_ref
                )


def turn_kernel(weights, rectangles, width, partner_ref, ranks_ref, factors_ref, held_ref,
                incoming_ref, base_ref, lower_ref, previous_ref, *rest):
    if weights is None:
        residual_ref, *rest = rest
        buffer, semaphore, split_ref, received_ref, turned_ref = rest
    else:
        residual_ref, direction_ref, outgoing_ref, *rest = rest
        buffer, semaphore, split_ref, received_ref, turned_ref, sums_ref = rest
    pieces = Pieces(rectangles, factors_ref, buffer, semaphore, split_ref, held_ref)
    pieces.start()
    unpack(width, factors_ref.shape[0] // width, partner_ref, incoming_ref, received_ref)
    turned_ref[...] = received_ref[...].T
    rows = factors_ref.shape[0]
    for index, ((first, last), columns) in enumerate(rectangles):
        @apart(partner_ref)
        def _():
            block = slice(*columns)
            pieces.load(index)
            if first == 0:
                before = base_ref[:, block] - lower_ref[:, block]
            else:
                before = residual_ref[:, block]
            residual = before - pieces.far(index, turned_ref)
            residual_ref[:, block] = residual
            if weights is None or last < rows:
                return
            old, new = weights
            direction = new * residual
            if old is not None:
                direction = old * previous_ref[:, block] + direction
            direction_ref[:, block] = direction
            if index + 1 < len(rectangles):
                project(split_ref, direction, sums_ref, columns[0] == 0)
            else:
                project_last(
                    split_ref, direction, sums_ref, width, partner_ref, ranks_ref, outgoing_ref
                )


SMEM_SPEC = pl.BlockSpec(memory_space=pltpu.SMEM)
VMEM_SPEC = pl.BlockSpec(memory_space=pltpu.VMEM)
ANY_SPEC = pl.BlockSpec(memory_space=pltpu.HBM)


def body(right_side, start, diag_tiles, neighbour_tiles, factors, partner, ranks):
    device_count = lax.axis_size(AXES)
    right_side, start = right_side[0], start[0]
    diag_block, neighbour_block, factor_block = diag_tiles[0], neighbour_tiles[0], factors[0]
    partner, ranks = partner[0], ranks[0]
    slots, rank_width, points = factor_block.shape
    n = start.shape[0]
    rows = slots * rank_width
    block = jax.ShapeDtypeStruct((n, points), jnp.float32)
    chunks = jax.ShapeDtypeStruct((device_count, rank_width // 2, 2 * n), jnp.float32)
    factor_block = factor_block.reshape(rows, points)
    middle, quarter = points // 2, points // 4
    by_columns = [((0, rows), (at, at + quarter)) for at in range(0, points, quarter)]
    held_rows = 512
    held = factor_block[:held_rows, :middle]
    factor_block = pltpu.with_memory_space_constraint(factor_block, pltpu.HBM)
    left = [(0, held_rows)] + [
        (held_rows + first, held_rows + last) for first, last in cuts(rows - held_rows, 3)
    ]
    left = [(part, (0, middle)) for part in left]
    by_halves = left + [((0, rows), (middle, points))]
    for_last = left + [((0, rows), (middle, middle + quarter))] + [
        (part, (middle + quarter, points)) for part in cuts(rows, 2)
    ]

    def loading(rectangles):
        width = max(right - left for _, (left, right) in rectangles)
        return [
            pltpu.VMEM((rows, points), jnp.float32),
            pltpu.SemaphoreType.DMA((len(rectangles),)),
            pltpu.VMEM((rows, 2 * width), jnp.bfloat16),
        ]

    received = [
        pltpu.VMEM((rows, 2 * n), jnp.bfloat16),
        pltpu.VMEM((2 * n, rows), jnp.bfloat16),
    ]
    sums = pltpu.VMEM((rows, 2 * n), jnp.float32)
    params = pltpu.CompilerParams(vmem_limit_bytes=VMEM_LIMIT)

    def cost(times):
        return pl.CostEstimate(
            flops=times * 8 * rows * points * n, bytes_accessed=4 * rows * points,
            transcendentals=0,
        )

    def in_place(array):
        return pltpu.with_memory_space_constraint(array, pltpu.HBM)

    def projected(vectors):
        return pl.pallas_call(
            functools.partial(project_kernel, by_columns, rank_width),
            out_shape=chunks,
            in_specs=[ANY_SPEC] * 4,
            out_specs=VMEM_SPEC,
            scratch_shapes=loading(by_columns) + [
                sums,
                pltpu.SMEM((slots,), jnp.int32),
                pltpu.SMEM((slots,), jnp.int32),
                pltpu.VMEM((n, points), jnp.float32),
                pltpu.SemaphoreType.DMA((3,)),
            ],
            compiler_params=params,
            cost_estimate=cost(1),
            name="project",
        )(in_place(partner), in_place(ranks), in_place(vectors), factor_block)

    def turn(weights, incoming, base, lower, previous):
        last = weights is None
        rectangles = for_last if last else by_halves
        outs = (block,) if last else (block, block, chunks)
        return pl.pallas_call(
            functools.partial(turn_kernel, weights, rectangles, rank_width),
            out_shape=outs,
            in_specs=[SMEM_SPEC, SMEM_SPEC, ANY_SPEC] + [VMEM_SPEC] * 5,
            out_specs=(VMEM_SPEC,) * len(outs),
            scratch_shapes=loading(rectangles) + received + ([] if last else [sums]),
            compiler_params=params,
            cost_estimate=cost(1 if last else 2),
            name="far" if last else "turn",
        )(partner, ranks, factor_block, held, incoming, base, lower, previous)

    def finish(outgoing, vectors, before, weights):
        exact = lax.Precision.HIGH
        incoming = lax.all_to_all(
            outgoing, AXES, split_axis=0, concat_axis=0, tiled=True
        )
        following = []
        for part in jnp.split(vectors, 2, axis=1):
            following.append(from_behind(part, -1))
        carried = lax.dot_general(vectors, neighbour_block, NN, precision=exact)
        lower_term = from_behind(carried, 1)
        partial = before - lax.dot_general(vectors, diag_block, NT, precision=exact)
        partial = lax.optimization_barrier(partial)
        for part, tile in zip(following, jnp.split(neighbour_block, 2, axis=1)):
            partial = lax.optimization_barrier(
                partial - lax.dot_general(part, tile, NT, precision=exact)
            )
        return turn(weights, incoming, partial, lower_term, vectors)

    center = (spectrum_low + spectrum_high) / 2.0
    half_width = (spectrum_high - spectrum_low) / 2.0
    ratio = center / half_width
    rho_now = 1.0 / ratio
    solution = start
    outgoing = projected(start)
    residual, direction, outgoing = finish(outgoing, start, right_side, (None, 1.0 / center))
    for iteration in range(ITERS):
        solution = solution + direction
        if iteration + 1 < ITERS:
            rho_next = 1.0 / (2.0 * ratio - rho_now)
            weights = (rho_next * rho_now, 2.0 * rho_next / half_width)
            residual, direction, outgoing = finish(outgoing, direction, residual, weights)
            rho_now = rho_next
        else:
            (residual,) = finish(outgoing, direction, residual, None)
    return (solution[None], residual[None])


def solution(mesh):
    return jax.shard_map(
        body,
        mesh=mesh,
        in_specs=(
            P(AXES, None, None),
            P(AXES, None, None),
            P(AXES, None, None),
            P(AXES, None, None),
            P(AXES, None, None, None),
            P(AXES, None),
            P(AXES, None),
        ),
        out_specs=(P(AXES, None, None), P(AXES, None, None)),
        check_vma=False,
    )
```

```python
import functools

import jax
import jax.numpy as jnp
from jax import lax
from jax.experimental import pallas as pl
from jax.experimental.pallas import tpu as pltpu
from jax.sharding import PartitionSpec as P


ITERS = 2

spectrum_low = 0.7
spectrum_high = 3.6

AXES = ("chain", "grp")
NT = (((1,), (1,)), ((), ()))
NN = (((1,), (0,)), ((), ()))
VMEM_LIMIT = 40 * 1024 * 1024


def from_behind(block, distance):
    devices = range(lax.axis_size(AXES))
    route = [(i - distance, i) for i in devices if i - distance in devices]
    return lax.ppermute(block, AXES, route)


def halves(value):
    high = value.astype(jnp.bfloat16)
    low = (value - high.astype(jnp.float32)).astype(jnp.bfloat16)
    return high, low


def product(left, right, form):
    return lax.dot_general(left, right, form, preferred_element_type=jnp.float32)


def cuts(rows, parts):
    edges = [rows * part // parts // 256 * 256 for part in range(parts)] + [rows]
    return [(first, last) for first, last in zip(edges, edges[1:]) if last > first]


class Pieces:
    def __init__(self, rectangles, factors_ref, buffer, semaphore, split_ref, held_ref=None):
        self.rectangles, self.factors_ref, self.buffer = rectangles, factors_ref, buffer
        self.semaphore, self.split_ref, self.held_ref = semaphore, split_ref, held_ref

    def held(self, index):
        return index == 0 and self.held_ref is not None

    def copy(self, index):
        rows, columns = (slice(*edges) for edges in self.rectangles[index])
        return pltpu.make_async_copy(
            self.factors_ref.at[rows, columns], self.buffer.at[rows, columns],
            self.semaphore.at[index],
        )

    def start(self):
        for index in range(len(self.rectangles)):
            if not self.held(index):
                self.copy(index).start()

    def load(self, index):
        rows, columns = (slice(*edges) for edges in self.rectangles[index])
        if self.held(index):
            values = self.held_ref[...]
        else:
            self.copy(index).wait()
            values = self.buffer[rows, columns]
        high, low = halves(values)
        width = high.shape[1]
        self.split_ref[rows, :width], self.split_ref[rows, width:2 * width] = high, low

    def far(self, index, turned_ref):
        (first, last), (left, right) = self.rectangles[index]
        width = right - left
        total = product(turned_ref[:, first:last], self.split_ref[first:last, :2 * width], NN)
        n = total.shape[0] // 2
        total = total[:n] + total[n:]
        return total[:, :width] + total[:, width:]


def operand_of(vectors):
    operand = jnp.concatenate(halves(vectors), axis=0).T
    return jnp.concatenate([operand, operand], axis=0)


def project(split_ref, vectors, sums_ref, first):
    total = product(split_ref[:, :2 * vectors.shape[1]], operand_of(vectors), NN)
    sums_ref[...] = total if first else sums_ref[...] + total


def store_chunks(slots, total, width, partner_ref, ranks_ref, outgoing_ref):
    lanes = total.shape[1]
    half = width // 2
    own = lax.axis_index(AXES)
    left = lax.broadcasted_iota(jnp.int32, (half, lanes), 1) < lanes // 2
    rank_index = lax.broadcasted_iota(jnp.int32, (half, lanes), 0) + jnp.where(left, 0, half)
    total = total + pltpu.roll(total, lanes // 2, 1)
    for inner, slot in enumerate(slots):
        base = inner * width
        chunk = jnp.where(left, total[base:base + half], total[base + half:base + width])
        chunk = jnp.where(rank_index < ranks_ref[slot], chunk, 0.0)
        place = partner_ref[slot]
        outgoing_ref[jnp.where(place >= 0, place, own)] = chunk


def project_last(split_ref, vectors, sums_ref, width, partner_ref, ranks_ref, outgoing_ref):
    operand = operand_of(vectors)
    slots = sums_ref.shape[0] // width
    together = -(-slots // 4)
    for at in range(0, slots, together):
        end = min(at + together, slots)
        some = slice(at * width, end * width)
        total = sums_ref[some, :] + product(split_ref[some, :operand.shape[0]], operand, NN)
        store_chunks(range(at, end), total, width, partner_ref, ranks_ref, outgoing_ref)


def apart(partner_ref):
    return pl.when(partner_ref[0] >= -1)


def each_slot(slots, visit):
    together = next(size for size in (7, 4, 2, 1) if slots % size == 0)

    @pl.loop(0, slots // together)
    def _(group):
        for inner in range(together):
            visit(group * together + inner)


def unpack(width, slots, partner_ref, incoming_ref, received_ref):
    _, half, lanes = incoming_ref.shape
    n = lanes // 2
    left = lax.broadcasted_iota(jnp.int32, (half, lanes), 1) < n

    def visit(slot):
        place = partner_ref[slot]
        chunk = jnp.where(place >= 0, incoming_ref[jnp.maximum(place, 0)], 0.0)
        high = chunk.astype(jnp.bfloat16).astype(jnp.float32)
        low = chunk - high
        top = jnp.where(left, high, pltpu.roll(low, n, 1))
        bottom = jnp.where(left, pltpu.roll(high, n, 1), low)
        base = pl.multiple_of(slot * width, 16)
        received_ref[pl.ds(base, half), :] = top.astype(jnp.bfloat16)
        received_ref[pl.ds(base + half, half), :] = bottom.astype(jnp.bfloat16)

    each_slot(slots, visit)


def project_kernel(groups, width, partner_hbm, ranks_hbm, vectors_hbm, factors_ref,
                   outgoing_ref, buffer, semaphore, split_ref, partner_ref, ranks_ref,
                   vectors_ref, operand_ref, small_semaphore):
    small = [
        pltpu.make_async_copy(source, target, small_semaphore.at[index])
        for index, (source, target) in enumerate((
            (vectors_hbm, vectors_ref), (partner_hbm, partner_ref), (ranks_hbm, ranks_ref)
        ))
    ]
    for copy in small:
        copy.start()
    points = factors_ref.shape[1]
    rectangles = [((first * width, last * width), (0, points)) for first, last in groups]
    pieces = Pieces(rectangles, factors_ref, buffer, semaphore, None)
    pieces.start()
    for copy in small:
        copy.wait()
    operand_ref[...] = operand_of(vectors_ref[...])
    for index, (first, last) in enumerate(groups):
        rows = (last - first) * width

        @apart(partner_ref)
        def _():
            pieces.copy(index).wait()
            high, low = halves(buffer[first * width:last * width])
            split_ref[:rows, :points], split_ref[:rows, points:] = high, low
            total = product(split_ref[:rows, :], operand_ref[...], NN)
            store_chunks(
                range(first, last), total, width, partner_ref, ranks_ref, outgoing_ref
            )


def turn_kernel(weights, rectangles, width, partner_ref, ranks_ref, factors_ref, held_ref,
                incoming_ref, base_ref, lower_ref, previous_ref, *rest):
    if weights is None:
        residual_ref, *rest = rest
        buffer, semaphore, split_ref, received_ref, turned_ref = rest
    else:
        residual_ref, direction_ref, outgoing_ref, *rest = rest
        buffer, semaphore, split_ref, received_ref, turned_ref, sums_ref = rest
    pieces = Pieces(rectangles, factors_ref, buffer, semaphore, split_ref, held_ref)
    pieces.start()
    unpack(width, factors_ref.shape[0] // width, partner_ref, incoming_ref, received_ref)
    turned_ref[...] = received_ref[...].T
    rows = factors_ref.shape[0]
    for index, ((first, last), columns) in enumerate(rectangles):
        @apart(partner_ref)
        def _():
            block = slice(*columns)
            pieces.load(index)
            if first == 0:
                before = base_ref[:, block] - lower_ref[:, block]
            else:
                before = residual_ref[:, block]
            residual = before - pieces.far(index, turned_ref)
            residual_ref[:, block] = residual
            if weights is None or last < rows:
                return
            old, new = weights
            direction = new * residual
            if old is not None:
                direction = old * previous_ref[:, block] + direction
            direction_ref[:, block] = direction
            if index + 1 < len(rectangles):
                project(split_ref, direction, sums_ref, columns[0] == 0)
            else:
                project_last(
                    split_ref, direction, sums_ref, width, partner_ref, ranks_ref, outgoing_ref
                )


SMEM_SPEC = pl.BlockSpec(memory_space=pltpu.SMEM)
VMEM_SPEC = pl.BlockSpec(memory_space=pltpu.VMEM)
ANY_SPEC = pl.BlockSpec(memory_space=pltpu.HBM)


def body(right_side, start, diag_tiles, neighbour_tiles, factors, partner, ranks):
    device_count = lax.axis_size(AXES)
    right_side, start = right_side[0], start[0]
    diag_block, neighbour_block, factor_block = diag_tiles[0], neighbour_tiles[0], factors[0]
    partner, ranks = partner[0], ranks[0]
    slots, rank_width, points = factor_block.shape
    n = start.shape[0]
    rows = slots * rank_width
    block = jax.ShapeDtypeStruct((n, points), jnp.float32)
    chunks = jax.ShapeDtypeStruct((device_count, rank_width // 2, 2 * n), jnp.float32)
    factor_block = factor_block.reshape(rows, points)
    middle, quarter = points // 2, points // 4
    together = -(-slots // 2)
    groups = [(at, min(at + together, slots)) for at in range(0, slots, together)]
    held_rows = 512
    held = factor_block[:held_rows, :middle]
    factor_block = pltpu.with_memory_space_constraint(factor_block, pltpu.HBM)
    left = [(0, held_rows)] + [
        (held_rows + first, held_rows + last) for first, last in cuts(rows - held_rows, 3)
    ]
    left = [(part, (0, middle)) for part in left]
    by_halves = left + [((0, rows), (middle, points))]
    for_last = left + [((0, rows), (middle, middle + quarter))] + [
        (part, (middle + quarter, points)) for part in cuts(rows, 2)
    ]

    def loading(rectangles):
        width = max(right - left for _, (left, right) in rectangles)
        return [
            pltpu.VMEM((rows, points), jnp.float32),
            pltpu.SemaphoreType.DMA((len(rectangles),)),
            pltpu.VMEM((rows, 2 * width), jnp.bfloat16),
        ]

    received = [
        pltpu.VMEM((rows, 2 * n), jnp.bfloat16),
        pltpu.VMEM((2 * n, rows), jnp.bfloat16),
    ]
    sums = pltpu.VMEM((rows, 2 * n), jnp.float32)
    params = pltpu.CompilerParams(vmem_limit_bytes=VMEM_LIMIT)

    def cost(times):
        return pl.CostEstimate(
            flops=times * 8 * rows * points * n, bytes_accessed=4 * rows * points,
            transcendentals=0,
        )

    def in_place(array):
        return pltpu.with_memory_space_constraint(array, pltpu.HBM)

    def projected(vectors):
        return pl.pallas_call(
            functools.partial(project_kernel, groups, rank_width),
            out_shape=chunks,
            in_specs=[ANY_SPEC] * 4,
            out_specs=VMEM_SPEC,
            scratch_shapes=[
                pltpu.VMEM((rows, points), jnp.float32),
                pltpu.SemaphoreType.DMA((len(groups),)),
                pltpu.VMEM((together * rank_width, 2 * points), jnp.bfloat16),
                pltpu.SMEM((slots,), jnp.int32),
                pltpu.SMEM((slots,), jnp.int32),
                pltpu.VMEM((n, points), jnp.float32),
                pltpu.VMEM((2 * points, 2 * n), jnp.bfloat16),
                pltpu.SemaphoreType.DMA((3,)),
            ],
            compiler_params=params,
            cost_estimate=cost(1),
            name="project",
        )(in_place(partner), in_place(ranks), in_place(vectors), factor_block)

    def turn(weights, incoming, base, lower, previous):
        last = weights is None
        rectangles = for_last if last else by_halves
        outs = (block,) if last else (block, block, chunks)
        return pl.pallas_call(
            functools.partial(turn_kernel, weights, rectangles, rank_width),
            out_shape=outs,
            in_specs=[SMEM_SPEC, SMEM_SPEC, ANY_SPEC] + [VMEM_SPEC] * 5,
            out_specs=(VMEM_SPEC,) * len(outs),
            scratch_shapes=loading(rectangles) + received + ([] if last else [sums]),
            compiler_params=params,
            cost_estimate=cost(1 if last else 2),
            name="far" if last else "turn",
        )(partner, ranks, factor_block, held, incoming, base, lower, previous)

    def finish(outgoing, vectors, before, weights):
        exact = lax.Precision.HIGH
        incoming = lax.all_to_all(
            outgoing, AXES, split_axis=0, concat_axis=0, tiled=True
        )
        following = []
        for part in jnp.split(vectors, 2, axis=1):
            following.append(from_behind(part, -1))
        carried = lax.dot_general(vectors, neighbour_block, NN, precision=exact)
        lower_term = from_behind(carried, 1)
        partial = before - lax.dot_general(vectors, diag_block, NT, precision=exact)
        partial = lax.optimization_barrier(partial)
        for part, tile in zip(following, jnp.split(neighbour_block, 2, axis=1)):
            partial = lax.optimization_barrier(
                partial - lax.dot_general(part, tile, NT, precision=exact)
            )
        return turn(weights, incoming, partial, lower_term, vectors)

    center = (spectrum_low + spectrum_high) / 2.0
    half_width = (spectrum_high - spectrum_low) / 2.0
    ratio = center / half_width
    rho_now = 1.0 / ratio
    solution = start
    outgoing = projected(start)
    residual, direction, outgoing = finish(outgoing, start, right_side, (None, 1.0 / center))
    for iteration in range(ITERS):
        solution = solution + direction
        if iteration + 1 < ITERS:
            rho_next = 1.0 / (2.0 * ratio - rho_now)
            weights = (rho_next * rho_now, 2.0 * rho_next / half_width)
            residual, direction, outgoing = finish(outgoing, direction, residual, weights)
            rho_now = rho_next
        else:
            (residual,) = finish(outgoing, direction, residual, None)
    return (solution[None], residual[None])


def solution(mesh):
    return jax.shard_map(
        body,
        mesh=mesh,
        in_specs=(
            P(AXES, None, None),
            P(AXES, None, None),
            P(AXES, None, None),
            P(AXES, None, None),
            P(AXES, None, None, None),
            P(AXES, None),
            P(AXES, None),
        ),
        out_specs=(P(AXES, None, None), P(AXES, None, None)),
        check_vma=False,
    )
```

```python
import functools

import jax
import jax.numpy as jnp
from jax import lax
from jax.experimental import pallas as pl
from jax.experimental.pallas import tpu as pltpu
from jax.sharding import PartitionSpec as P


ITERS = 2

spectrum_low = 0.7
spectrum_high = 3.6

AXES = ("chain", "grp")
NT = (((1,), (1,)), ((), ()))
NN = (((1,), (0,)), ((), ()))
VMEM_LIMIT = 40 * 1024 * 1024


def from_behind(block, distance):
    devices = range(lax.axis_size(AXES))
    route = [(i - distance, i) for i in devices if i - distance in devices]
    return lax.ppermute(block, AXES, route)


def halves(value):
    high = value.astype(jnp.bfloat16)
    low = (value - high.astype(jnp.float32)).astype(jnp.bfloat16)
    return high, low


def product(left, right, form):
    return lax.dot_general(left, right, form, preferred_element_type=jnp.float32)


def cuts(rows, parts):
    edges = [rows * part // parts // 256 * 256 for part in range(parts)] + [rows]
    return [(first, last) for first, last in zip(edges, edges[1:]) if last > first]


class Pieces:
    def __init__(self, rectangles, factors_ref, buffer, semaphore, split_ref, held_ref=None):
        self.rectangles, self.factors_ref, self.buffer = rectangles, factors_ref, buffer
        self.semaphore, self.split_ref, self.held_ref = semaphore, split_ref, held_ref

    def held(self, index):
        return index == 0 and self.held_ref is not None

    def copy(self, index):
        rows, columns = (slice(*edges) for edges in self.rectangles[index])
        return pltpu.make_async_copy(
            self.factors_ref.at[rows, columns], self.buffer.at[rows, columns],
            self.semaphore.at[index],
        )

    def start(self):
        for index in range(len(self.rectangles)):
            if not self.held(index):
                self.copy(index).start()

    def load(self, index):
        rows, columns = (slice(*edges) for edges in self.rectangles[index])
        if self.held(index):
            values = self.held_ref[...]
        else:
            self.copy(index).wait()
            values = self.buffer[rows, columns]
        high, low = halves(values)
        width = high.shape[1]
        self.split_ref[rows, :width], self.split_ref[rows, width:2 * width] = high, low

    def far(self, index, turned_ref):
        (first, last), (left, right) = self.rectangles[index]
        width = right - left
        total = product(turned_ref[:, first:last], self.split_ref[first:last, :2 * width], NN)
        n = total.shape[0] // 2
        total = total[:n] + total[n:]
        return total[:, :width] + total[:, width:]


def operand_of(vectors):
    operand = jnp.concatenate(halves(vectors), axis=0).T
    return jnp.concatenate([operand, operand], axis=0)


def project(split_ref, vectors, sums_ref, first):
    total = product(split_ref[:, :2 * vectors.shape[1]], operand_of(vectors), NN)
    sums_ref[...] = total if first else sums_ref[...] + total


def store_chunks(slots, total, width, partner_ref, ranks_ref, outgoing_ref):
    lanes = total.shape[1]
    half = width // 2
    own = lax.axis_index(AXES)
    left = lax.broadcasted_iota(jnp.int32, (half, lanes), 1) < lanes // 2
    rank_index = lax.broadcasted_iota(jnp.int32, (half, lanes), 0) + jnp.where(left, 0, half)
    total = total + pltpu.roll(total, lanes // 2, 1)
    for inner, slot in enumerate(slots):
        base = inner * width
        chunk = jnp.where(left, total[base:base + half], total[base + half:base + width])
        chunk = jnp.where(rank_index < ranks_ref[slot], chunk, 0.0)
        place = partner_ref[slot]
        outgoing_ref[jnp.where(place >= 0, place, own)] = chunk


def project_last(split_ref, vectors, sums_ref, width, partner_ref, ranks_ref, outgoing_ref):
    operand = operand_of(vectors)
    slots = sums_ref.shape[0] // width
    together = -(-slots // 2)
    for at in range(0, slots, together):
        end = min(at + together, slots)
        some = slice(at * width, end * width)
        total = sums_ref[some, :] + product(split_ref[some, :operand.shape[0]], operand, NN)
        store_chunks(range(at, end), total, width, partner_ref, ranks_ref, outgoing_ref)


def apart(partner_ref):
    return pl.when(partner_ref[0] >= -1)


def each_slot(slots, visit):
    together = next(size for size in (14, 11, 7, 4, 2, 1) if slots % size == 0)

    @pl.loop(0, slots // together)
    def _(group):
        for inner in range(together):
            visit(group * together + inner)


def unpack(width, slots, partner_ref, incoming_ref, received_ref):
    _, half, lanes = incoming_ref.shape
    n = lanes // 2
    left = lax.broadcasted_iota(jnp.int32, (half, lanes), 1) < n

    def visit(slot):
        place = partner_ref[slot]
        chunk = jnp.where(place >= 0, incoming_ref[jnp.maximum(place, 0)], 0.0)
        high = chunk.astype(jnp.bfloat16).astype(jnp.float32)
        low = chunk - high
        top = jnp.where(left, high, pltpu.roll(low, n, 1))
        bottom = jnp.where(left, pltpu.roll(high, n, 1), low)
        base = pl.multiple_of(slot * width, 16)
        received_ref[pl.ds(base, half), :] = top.astype(jnp.bfloat16)
        received_ref[pl.ds(base + half, half), :] = bottom.astype(jnp.bfloat16)

    each_slot(slots, visit)


def project_kernel(groups, width, partner_hbm, ranks_hbm, vectors_hbm, factors_ref,
                   outgoing_ref, buffer, semaphore, split_ref, partner_ref, ranks_ref,
                   vectors_ref, operand_ref, small_semaphore):
    small = [
        pltpu.make_async_copy(source, target, small_semaphore.at[index])
        for index, (source, target) in enumerate((
            (vectors_hbm, vectors_ref), (partner_hbm, partner_ref), (ranks_hbm, ranks_ref)
        ))
    ]
    for copy in small:
        copy.start()
    points = factors_ref.shape[1]
    rectangles = [((first * width, last * width), (0, points)) for first, last in groups]
    pieces = Pieces(rectangles, factors_ref, buffer, semaphore, None)
    pieces.start()
    for copy in small:
        copy.wait()
    operand_ref[...] = operand_of(vectors_ref[...])
    for index, (first, last) in enumerate(groups):
        rows = (last - first) * width

        @apart(partner_ref)
        def _():
            pieces.copy(index).wait()
            high, low = halves(buffer[first * width:last * width])
            split_ref[:rows, :points], split_ref[:rows, points:] = high, low
            total = product(split_ref[:rows, :], operand_ref[...], NN)
            store_chunks(
                range(first, last), total, width, partner_ref, ranks_ref, outgoing_ref
            )


def turn_kernel(weights, rectangles, width, partner_hbm, ranks_hbm, factors_ref, held_ref,
                incoming_ref, base_ref, lower_ref, previous_ref, *rest):
    *rest, partner_ref, ranks_ref, small_semaphore = rest
    if weights is None:
        residual_ref, *rest = rest
        buffer, semaphore, split_ref, received_ref, turned_ref = rest
    else:
        residual_ref, direction_ref, outgoing_ref, *rest = rest
        buffer, semaphore, split_ref, received_ref, turned_ref, sums_ref = rest
    small = [
        pltpu.make_async_copy(source, target, small_semaphore.at[index])
        for index, (source, target) in enumerate((
            (partner_hbm, partner_ref), (ranks_hbm, ranks_ref)
        ))
    ]
    for copy in small:
        copy.start()
    pieces = Pieces(rectangles, factors_ref, buffer, semaphore, split_ref, held_ref)
    pieces.start()
    for copy in small:
        copy.wait()
    unpack(width, factors_ref.shape[0] // width, partner_ref, incoming_ref, received_ref)
    turned_ref[...] = received_ref[...].T
    rows = factors_ref.shape[0]
    for index, ((first, last), columns) in enumerate(rectangles):
        @apart(partner_ref)
        def _():
            block = slice(*columns)
            pieces.load(index)
            if first == 0:
                before = base_ref[:, block] - lower_ref[:, block]
            else:
                before = residual_ref[:, block]
            residual = before - pieces.far(index, turned_ref)
            residual_ref[:, block] = residual
            if weights is None or last < rows:
                return
            old, new = weights
            direction = new * residual
            if old is not None:
                direction = old * previous_ref[:, block] + direction
            direction_ref[:, block] = direction
            if index + 1 < len(rectangles):
                project(split_ref, direction, sums_ref, columns[0] == 0)
            else:
                project_last(
                    split_ref, direction, sums_ref, width, partner_ref, ranks_ref, outgoing_ref
                )


VMEM_SPEC = pl.BlockSpec(memory_space=pltpu.VMEM)
ANY_SPEC = pl.BlockSpec(memory_space=pltpu.HBM)


def body(right_side, start, diag_tiles, neighbour_tiles, factors, partner, ranks):
    device_count = lax.axis_size(AXES)
    right_side, start = right_side[0], start[0]
    diag_block, neighbour_block, factor_block = diag_tiles[0], neighbour_tiles[0], factors[0]
    partner, ranks = partner[0], ranks[0]
    slots, rank_width, points = factor_block.shape
    n = start.shape[0]
    rows = slots * rank_width
    block = jax.ShapeDtypeStruct((n, points), jnp.float32)
    chunks = jax.ShapeDtypeStruct((device_count, rank_width // 2, 2 * n), jnp.float32)
    factor_block = factor_block.reshape(rows, points)
    middle, quarter = points // 2, points // 4
    together = -(-slots // 2)
    groups = [(at, min(at + together, slots)) for at in range(0, slots, together)]
    held_rows = 512
    held = factor_block[:held_rows, :middle]
    factor_block = pltpu.with_memory_space_constraint(factor_block, pltpu.HBM)
    left = [(0, held_rows)] + [
        (held_rows + first, held_rows + last) for first, last in cuts(rows - held_rows, 3)
    ]
    left = [(part, (0, middle)) for part in left]
    by_halves = left + [((0, rows), (middle, points))]
    for_last = left + [((0, rows), (middle, middle + quarter))] + [
        (part, (middle + quarter, points)) for part in cuts(rows, 2)
    ]

    def loading(rectangles):
        width = max(right - left for _, (left, right) in rectangles)
        return [
            pltpu.VMEM((rows, points), jnp.float32),
            pltpu.SemaphoreType.DMA((len(rectangles),)),
            pltpu.VMEM((rows, 2 * width), jnp.bfloat16),
        ]

    received = [
        pltpu.VMEM((rows, 2 * n), jnp.bfloat16),
        pltpu.VMEM((2 * n, rows), jnp.bfloat16),
    ]
    sums = pltpu.VMEM((rows, 2 * n), jnp.float32)
    params = pltpu.CompilerParams(vmem_limit_bytes=VMEM_LIMIT)

    def cost(times):
        return pl.CostEstimate(
            flops=times * 8 * rows * points * n, bytes_accessed=4 * rows * points,
            transcendentals=0,
        )

    def in_place(array):
        return pltpu.with_memory_space_constraint(array, pltpu.HBM)

    def projected(vectors):
        return pl.pallas_call(
            functools.partial(project_kernel, groups, rank_width),
            out_shape=chunks,
            in_specs=[ANY_SPEC] * 4,
            out_specs=VMEM_SPEC,
            scratch_shapes=[
                pltpu.VMEM((rows, points), jnp.float32),
                pltpu.SemaphoreType.DMA((len(groups),)),
                pltpu.VMEM((together * rank_width, 2 * points), jnp.bfloat16),
                pltpu.SMEM((slots,), jnp.int32),
                pltpu.SMEM((slots,), jnp.int32),
                pltpu.VMEM((n, points), jnp.float32),
                pltpu.VMEM((2 * points, 2 * n), jnp.bfloat16),
                pltpu.SemaphoreType.DMA((3,)),
            ],
            compiler_params=params,
            cost_estimate=cost(1),
            name="project",
        )(in_place(partner), in_place(ranks), in_place(vectors), factor_block)

    def turn(weights, incoming, base, lower, previous):
        last = weights is None
        rectangles = for_last if last else by_halves
        outs = (block,) if last else (block, block, chunks)
        return pl.pallas_call(
            functools.partial(turn_kernel, weights, rectangles, rank_width),
            out_shape=outs,
            in_specs=[pl.BlockSpec(memory_space=pl.ANY)] * 2 + [ANY_SPEC] + [VMEM_SPEC] * 5,
            out_specs=(VMEM_SPEC,) * len(outs),
            scratch_shapes=loading(rectangles) + received + ([] if last else [sums]) + [
                pltpu.SMEM((slots,), jnp.int32),
                pltpu.SMEM((slots,), jnp.int32),
                pltpu.SemaphoreType.DMA((2,)),
            ],
            compiler_params=params,
            cost_estimate=cost(1 if last else 2),
            name="far" if last else "turn",
        )(partner, ranks, factor_block, held, incoming, base, lower, previous)

    def finish(outgoing, vectors, before, weights):
        exact = lax.Precision.HIGH
        incoming = lax.all_to_all(
            outgoing, AXES, split_axis=0, concat_axis=0, tiled=True
        )
        following = []
        for part in jnp.split(vectors, 2, axis=1):
            following.append(from_behind(part, -1))
        carried = lax.dot_general(vectors, neighbour_block, NN, precision=exact)
        lower_term = from_behind(carried, 1)
        partial = before - lax.dot_general(vectors, diag_block, NT, precision=exact)
        partial = lax.optimization_barrier(partial)
        for part, tile in zip(following, jnp.split(neighbour_block, 2, axis=1)):
            partial = lax.optimization_barrier(
                partial - lax.dot_general(part, tile, NT, precision=exact)
            )
        return turn(weights, incoming, partial, lower_term, vectors)

    center = (spectrum_low + spectrum_high) / 2.0
    half_width = (spectrum_high - spectrum_low) / 2.0
    ratio = center / half_width
    rho_now = 1.0 / ratio
    solution = start
    outgoing = projected(start)
    residual, direction, outgoing = finish(outgoing, start, right_side, (None, 1.0 / center))
    for iteration in range(ITERS):
        solution = solution + direction
        if iteration + 1 < ITERS:
            rho_next = 1.0 / (2.0 * ratio - rho_now)
            weights = (rho_next * rho_now, 2.0 * rho_next / half_width)
            residual, direction, outgoing = finish(outgoing, direction, residual, weights)
            rho_now = rho_next
        else:
            (residual,) = finish(outgoing, direction, residual, None)
    return (solution[None], residual[None])


def solution(mesh):
    return jax.shard_map(
        body,
        mesh=mesh,
        in_specs=(
            P(AXES, None, None),
            P(AXES, None, None),
            P(AXES, None, None),
            P(AXES, None, None),
            P(AXES, None, None, None),
            P(AXES, None),
            P(AXES, None),
        ),
        out_specs=(P(AXES, None, None), P(AXES, None, None)),
        check_vma=False,
    )
```
